32 devices in a mesh: groups: 2 (over y), nodes: 4 (over z), heads: 2 (over x), sub: 2 (over core).
Axes of the slice: x: 2, y: 2, z: 4, core: 2. Of those that a mesh axis runs over, the one named last changes fastest.
Arguments:
- queries: bfloat16 [4096, 512], P(('groups', 'nodes', 'sub'), 'heads'), parts along dimension 0, may hold values from -60 to 60
- key_vectors: bfloat16 [4096, 512], P(('groups', 'nodes', 'sub'), 'heads'), parts along dimension 0, may hold values from -20 to 20
- value_vectors: bfloat16 [4096, 512], P(('groups', 'nodes', 'sub'), 'heads'), parts along dimension 0, may hold values from -6 to 6
- cotangent: bfloat16 [4096, 512], P(('groups', 'nodes', 'sub'), 'heads'), parts along dimension 0, may hold values from -6 to 6
- out_weight: bfloat16 [512, 512], P('heads'), may hold values from -0.25 to 0.25
- neighbours: int32 [32, 16], P('groups'), parts along dimension 0, may hold values from 0 to 15, as said below
- entry_mask: int32 [32, 16], P('groups'), parts along dimension 0, may hold values from 0 to 1, as said below
- live_counts: int32 [16], P('groups'), parts along dimension 0, may hold values from 1 to 2, as said below
- tile_slot: int32 [32], P('groups'), parts along dimension 0, may hold values from 0 to 15, as said below
Outputs:
- query_grad: bfloat16 [4096, 512], P(('groups', 'nodes', 'sub'), 'heads'), parts along dimension 0
- key_grad: bfloat16 [4096, 512], P(('groups', 'nodes', 'sub'), 'heads'), parts along dimension 0
- value_grad: bfloat16 [4096, 512], P(('groups', 'nodes', 'sub'), 'heads'), parts along dimension 0
- weight_grad: float32 [1024, 512], P(('groups', 'heads')), parts along dimension 0
The draws below stay inside these ranges and needn't reach their ends.
There are 2 independent parts, one for each index of `groups`. The reference program is written for one: setup_inputs(seed, part) draws one part's arguments, and reference() takes and returns one part's arrays. A program takes and returns all parts, laid end to end along the dimension named above; an argument that names none is the same for every part. Nothing has to cross between parts.
Inputs may be any that keep to these rules, and one draw needn't show every extreme that they name: `neighbours`: row r lists graph tiles for the query tile in slot r. Entry 0 is that tile itself; entries 1 to 7 name live tiles of the same shard; entries 8 to 15 name live tiles of the shards next to it (shard index one lower or one higher, none past either end). Entries may repeat. Over all rows of one shard, the entries name at most one distinct tile of each adjacent shard, and in every draw some shard names exactly one tile of an adjacent shard. `entry_mask`: entry 0 of every row is 1. The live tiles of shard s are its slots s * 2 to s * 2 + live_counts[s] - 1; at least one shard is full. `tile_slot`: the graph tiles g with g // 2 = s are held in the slots of shard s, each slot once.
All inputs are finite; a program needn't handle non-finite values.
Results may differ from the reference program's by a relative error of at most 0.025.
Values may be sent and summed in bfloat16 or wider, within the bound.
A program may use at most 64 MiB of HBM per device.

```python
import jax
import jax.numpy as jnp
from jax import lax

D = 512
HEADS = 8
HD = 64
TILE = 128
TILES_DEV = 2
DEG_IN = 8
DEG_OUT = 8
DEG = 16
HALO_CAP = 1
SHARDS = 8
TILES = 16
NODES = 2048


def query_key_pair(base_key):
    folded = jax.random.fold_in(base_key, 101)
    query_key, vector_key = jax.random.split(folded, 2)
    key_base = jnp.clip(jax.random.normal(vector_key, (NODES, D), jnp.float32), -4.0, 4.0) * 1.25
    query_base = jnp.clip(jax.random.normal(query_key, (NODES, D), jnp.float32), -4.0, 4.0) * 1.25
    return (query_base, key_base)


def tile_graph(base_key):
    folded = jax.random.fold_in(base_key, 202)
    count_key, full_key, perm_key, inner_key, side_key, pick_key, order_key, mask_key = jax.random.split(folded, 8)
    shard_range = jnp.arange(SHARDS, dtype=jnp.int32)
    tile_range = jnp.arange(TILES_DEV, dtype=jnp.int32)
    lowest = max(1, TILES_DEV // 4)
    counts = jax.random.randint(count_key, (SHARDS,), lowest, TILES_DEV + 1)
    full_shard = jax.random.randint(full_key, (), 0, SHARDS)
    counts = jnp.where(shard_range == full_shard, TILES_DEV, counts).astype(jnp.int32)
    orders = jax.random.randint(perm_key, (SHARDS, TILES_DEV), 0, 1 << 16) * TILES_DEV + tile_range[None, :]
    local_of_graph = jnp.argsort(orders, axis=1).astype(jnp.int32)
    tile_slot = (shard_range[:, None] * TILES_DEV + local_of_graph).reshape(TILES).astype(jnp.int32)
    graph_of_local = jnp.argsort(local_of_graph, axis=1).astype(jnp.int32)
    graph_of_slot = (shard_range[:, None] * TILES_DEV + graph_of_local).reshape(TILES)
    own_entry = graph_of_slot.reshape(SHARDS, TILES_DEV, 1)
    inner_local = jax.random.randint(inner_key, (SHARDS, TILES_DEV, DEG_IN - 1), 0, 1 << 20) % counts[:, None, None]
    inner_entries = jnp.take(graph_of_slot, shard_range[:, None, None] * TILES_DEV + inner_local)
    below_count = jnp.take(counts, jnp.maximum(shard_range - 1, 0))
    above_count = jnp.take(counts, jnp.minimum(shard_range + 1, SHARDS - 1))
    side_counts = jnp.stack([below_count, above_count], axis=1)
    ranking = jax.random.randint(order_key, (SHARDS, 2, TILES_DEV), 0, 1 << 16) * TILES_DEV + tile_range[None, None, :]
    ranking = ranking + (tile_range[None, None, :] >= side_counts[:, :, None]).astype(jnp.int32) * (1 << 24)
    chosen_sets = jnp.argsort(ranking, axis=2)[:, :, :HALO_CAP].astype(jnp.int32)
    set_sizes = jnp.minimum(side_counts, HALO_CAP)
    flat_pick = jnp.arange(TILES_DEV * DEG_OUT, dtype=jnp.int32).reshape(TILES_DEV, DEG_OUT)
    covering = flat_pick < 2 * HALO_CAP
    random_side = jax.random.randint(side_key, (SHARDS, TILES_DEV, DEG_OUT), 0, 2)
    side_bit = jnp.where(covering[None], flat_pick[None] % 2, random_side)
    side_bit = jnp.where(shard_range[:, None, None] == 0, 1, side_bit)
    side_bit = jnp.where(shard_range[:, None, None] == SHARDS - 1, 0, side_bit)
    size_here = jnp.where(side_bit == 1, set_sizes[:, 1][:, None, None], set_sizes[:, 0][:, None, None])
    random_pick = jax.random.randint(pick_key, (SHARDS, TILES_DEV, DEG_OUT), 0, 1 << 20)
    element = jnp.where(covering[None], flat_pick[None] // 2, random_pick) % size_here
    set_index = (shard_range[:, None, None] * 2 + side_bit) * HALO_CAP + element
    local_pick = jnp.take(chosen_sets.reshape(-1), set_index)
    adjacent = shard_range[:, None, None] + 2 * side_bit - 1
    outer_entries = jnp.take(graph_of_slot, adjacent * TILES_DEV + local_pick)
    neighbours = jnp.concatenate([own_entry, inner_entries, outer_entries], axis=2).reshape(TILES, DEG).astype(jnp.int32)
    entry_mask = (jax.random.randint(mask_key, (TILES, DEG), 0, 4) < 3).astype(jnp.int32)
    entry_mask = entry_mask.at[:, 0].set(1)
    return (neighbours, entry_mask, counts, tile_slot)


def draw_queries(key, part):
    return query_key_pair(key)[0].astype(jnp.bfloat16)


def draw_key_vectors(key, part):
    return query_key_pair(key)[1].astype(jnp.bfloat16)


def draw_neighbours(key, part):
    return tile_graph(key)[0]


def draw_entry_mask(key, part):
    return tile_graph(key)[1]


def draw_live_counts(key, part):
    return tile_graph(key)[2]


def draw_tile_slot(key, part):
    return tile_graph(key)[3]


def level_of(rng, shape, cuts, least, largest):
    level = 1.0
    for axis_at, blocks in cuts:
        heights = jax.random.uniform(jax.random.fold_in(jax.random.fold_in(rng, 6), axis_at), (blocks,), jnp.float32, least / len(cuts), largest / len(cuts))
        level = level * jnp.repeat(jnp.exp(heights), shape[axis_at] // blocks).reshape((-1,) + (1,) * (len(shape) - 1 - axis_at))
    return level


def gaussian(own_key, dims, deviation, most, cuts=(), kind=jnp.bfloat16):
    gain = level_of(own_key, dims, cuts, -0.22, 0.18) if cuts else 1.0
    drawn = jax.random.normal(own_key, dims, jnp.float32) * deviation * gain
    return jnp.minimum(jnp.maximum(drawn, -most), most).astype(kind)


def setup_inputs(seed: int = 0, part: int = 0) -> dict:
    keys = jax.random.split(jax.random.key(seed), 10)
    part_keys = jax.random.split(jax.random.fold_in(keys[9], part), 10)
    return {
        "queries": draw_queries(jax.random.fold_in(jax.random.fold_in(keys[9], part), 71), part),
        "key_vectors": draw_key_vectors(jax.random.fold_in(jax.random.fold_in(keys[9], part), 71), part),
        "value_vectors": gaussian(part_keys[2], (NODES, D), 1.0, 6.0, ((0, 8), (1, 2))),
        "cotangent": gaussian(part_keys[3], (NODES, D), 1.0, 6.0, ((0, 8), (1, 2))),
        "out_weight": gaussian(keys[4], (D, D), D ** -0.5, 0.25, ((0, 2),)),
        "neighbours": draw_neighbours(jax.random.fold_in(jax.random.fold_in(keys[9], part), 71), part),
        "entry_mask": draw_entry_mask(jax.random.fold_in(jax.random.fold_in(keys[9], part), 71), part),
        "live_counts": draw_live_counts(jax.random.fold_in(jax.random.fold_in(keys[9], part), 71), part),
        "tile_slot": draw_tile_slot(jax.random.fold_in(jax.random.fold_in(keys[9], part), 71), part),
    }


def tile_terms(query_heads, grad_heads, key_heads, value_heads, usable, living):
    head_size = query_heads.shape[-1]
    scaling = head_size ** -0.5
    scores = jnp.einsum("athd,aeshd->ahtes", query_heads, key_heads) * scaling
    visible = usable[:, None, None, :, None]
    scores = jnp.where(visible, scores, -1e30)
    topmost = jnp.max(scores, axis=(3, 4), keepdims=True)
    expanded = jnp.where(visible, jnp.exp(scores - topmost), 0.0)
    denominator = jnp.sum(expanded, axis=(3, 4), keepdims=True)
    denominator = jnp.where(living[:, None, None, None, None], denominator, 1.0)
    weights = expanded / denominator
    rounded = lax.optimization_barrier(weights.astype(jnp.bfloat16)).astype(jnp.float32)
    attended = jnp.einsum("ahtes,aeshd->athd", rounded, value_heads).astype(jnp.bfloat16)
    row_delta = jnp.sum(grad_heads * attended.astype(jnp.float32), axis=3)
    grad_scores = jnp.einsum("athd,aeshd->ahtes", grad_heads, value_heads)
    score_grad = weights * (grad_scores - jnp.transpose(row_delta, (0, 2, 1))[:, :, :, None, None]) * scaling
    score_half = lax.optimization_barrier(score_grad.astype(jnp.bfloat16)).astype(jnp.float32)
    query_part = jnp.einsum("ahtes,aeshd->athd", score_half, key_heads)
    key_part = jnp.einsum("ahtes,athd->aeshd", score_half, query_heads)
    value_part = jnp.einsum("ahtes,athd->aeshd", rounded, grad_heads)
    return query_part, attended, key_part, value_part


def reference(queries, key_vectors, value_vectors, cotangent, out_weight, neighbours, entry_mask, live_counts, tile_slot):
    out_grad = jnp.dot(cotangent, out_weight.T, preferred_element_type=jnp.float32).astype(jnp.bfloat16)
    tile_range = jnp.arange(TILES, dtype=jnp.int32)
    living = (tile_range % TILES_DEV) < jnp.take(live_counts, tile_range // TILES_DEV)
    usable = (entry_mask == 1) & living[:, None]
    key_slot = jnp.take(tile_slot, neighbours).astype(jnp.int32)
    tile_shape = (TILES, TILE, HEADS, HD)
    query_tiles = queries.astype(jnp.float32).reshape(tile_shape)
    key_tiles = key_vectors.astype(jnp.float32).reshape(tile_shape)
    value_tiles = value_vectors.astype(jnp.float32).reshape(tile_shape)
    grad_tiles = out_grad.astype(jnp.float32).reshape(tile_shape)
    pair_tiles = 2

    def advance(running, block_number):
        key_total, value_total = running
        first_tile = block_number * pair_tiles
        entries = lax.dynamic_slice_in_dim(key_slot, first_tile, pair_tiles, 0)
        query_part, attended, key_part, value_part = tile_terms(
            lax.dynamic_slice_in_dim(query_tiles, first_tile, pair_tiles, 0),
            lax.dynamic_slice_in_dim(grad_tiles, first_tile, pair_tiles, 0),
            jnp.take(key_tiles, entries, axis=0),
            jnp.take(value_tiles, entries, axis=0),
            lax.dynamic_slice_in_dim(usable, first_tile, pair_tiles, 0),
            lax.dynamic_slice_in_dim(living, first_tile, pair_tiles, 0))
        flat_entries = entries.reshape(-1)
        key_total = key_total.at[flat_entries].add(key_part.reshape(pair_tiles * DEG, TILE, HEADS, HD))
        value_total = value_total.at[flat_entries].add(value_part.reshape(pair_tiles * DEG, TILE, HEADS, HD))
        return (key_total, value_total), (query_part, attended)

    zero_tiles = jnp.zeros(tile_shape, jnp.float32)
    totals, outputs = lax.scan(advance, (zero_tiles, zero_tiles), jnp.arange(TILES // pair_tiles, dtype=jnp.int32))
    query_grad = outputs[0].reshape(NODES, D).astype(jnp.bfloat16)
    attended = outputs[1].reshape(NODES, D)
    key_grad = totals[0].reshape(NODES, D).astype(jnp.bfloat16)
    value_grad = totals[1].reshape(NODES, D).astype(jnp.bfloat16)
    weight_grad = jnp.dot(attended.T, cotangent, preferred_element_type=jnp.float32) * NODES ** -0.5
    return query_grad, key_grad, value_grad, weight_grad
```

```python
import functools

import jax
import jax.numpy as jnp
from jax import lax
from jax.experimental import pallas as pl
from jax.experimental.pallas import tpu as pltpu
from jax.sharding import PartitionSpec as P

HD = 64
TILE = 128
LANES = 128
HIDDEN = -1e30
MESH = pl.DeviceIdType.MESH
F32 = jnp.float32
BF16 = jnp.bfloat16


def mm(a, b):
    return jnp.dot(a, b, preferred_element_type=F32)


def mm_nt(a, b):
    return lax.dot_general(a, b, (((1,), (1,)), ((), ())), preferred_element_type=F32)


def turned(value):
    return jnp.transpose(value.astype(F32))


def kernel(
    sizes,
    nb_ref, mask_ref, live_ref, slot_ref,
    q_ref, k_ref, v_ref, cot_ref, w_ref,
    dq_ref, dk_ref, dv_ref, wg_ref,
    cotg, hsend, halo, gsend, grecv, qt, qm, dot_t, dom, kt, vt, att, pf, pb, sb, wsend, wrecv, zsend, zrecv, ag,
    x_send, x_recv, h_send, h_recv, g_send, g_recv, p_send, p_recv, z_send, z_recv, a_send, a_recv, f_send, f_recv,
):
    nz, nx, ns, owners = sizes
    rows, feats = q_ref.shape
    tiles = rows // TILE
    heads = feats // HD
    pairs = feats // LANES
    per = LANES // HD
    shards = nz * ns
    half = feats // ns
    piece = half // owners
    degree = nb_ref.shape[1]
    total_nodes = rows * shards
    z, x, c = lax.axis_index("nodes"), lax.axis_index("heads"), lax.axis_index("sub")
    s = z * ns + c
    up, down = jnp.minimum(s + 1, shards - 1), jnp.maximum(s - 1, 0)
    has = (s > 0, s < shards - 1)
    sides = (down, up)

    def at_shard(index):
        return {"nodes": lax.div(index, ns), "sub": lax.rem(index, ns)}

    def on_x(d):
        return lax.rem(x + d, nx)

    def on_z(d):
        return lax.rem(z + d, nz)

    def on_sub(d):
        return lax.rem(c + d, ns)

    cross = (jnp.logical_and(c == 0, z > 0), jnp.logical_and(c == ns - 1, z < nz - 1))

    barrier = pltpu.get_barrier_semaphore()

    def greet(device):
        pl.semaphore_signal(barrier, inc=1, device_id=device, device_id_type=MESH)

    for d in range(1, nx):
        greet({"heads": on_x(d)})
    for d in range(1, ns):
        greet({"sub": on_sub(d)})
    for side in range(2):
        @pl.when(cross[side])
        def _():
            greet(at_shard(sides[side]))
    for d in range(1, nz):
        greet({"nodes": on_z(d)})

    chosen = []
    for side in range(2):
        pick = jnp.int32(0)
        for r in range(tiles):
            for e in range(degree):
                slot = slot_ref[nb_ref[sides[side] * tiles + r, e]]
                local = slot - s * tiles
                inside = jnp.logical_and(local >= 0, local < tiles)
                pick = jnp.where(inside, local, pick)
        chosen.append(pick)
    for side in range(2):
        kk, vv = k_ref[0:TILE, :], v_ref[0:TILE, :]
        for t in range(1, tiles):
            here = chosen[side] == t
            kk = jnp.where(here, k_ref[t * TILE : (t + 1) * TILE, :], kk)
            vv = jnp.where(here, v_ref[t * TILE : (t + 1) * TILE, :], vv)
        hsend[side, 0] = kk
        hsend[side, 1] = vv

    extra = jnp.where(jnp.logical_or(cross[0], cross[1]), 1, 0)
    pl.semaphore_wait(barrier, nx - 1 + ns - 1 + nz - 1 + extra)

    def remote(src, dst, send, recv, device):
        return pltpu.make_async_remote_copy(
            src_ref=src, dst_ref=dst, send_sem=send, recv_sem=recv, device_id=device, device_id_type=MESH
        )

    def halo_copy(side):
        return remote(hsend.at[side], halo.at[1 - side], h_send.at[side], h_recv.at[1 - side], at_shard(sides[side]))

    def halo_wait(side):
        return remote(hsend.at[side], halo.at[side], h_send.at[side], h_recv.at[side], at_shard(sides[side]))

    def grad_copy(side):
        return remote(gsend.at[side], grecv.at[1 - side], g_send.at[side], g_recv.at[1 - side], at_shard(sides[side]))

    def grad_wait(side):
        return remote(gsend.at[side], grecv.at[side], g_send.at[side], g_recv.at[side], at_shard(sides[side]))

    for side in range(2):
        @pl.when(has[side])
        def _():
            halo_copy(side).start()

    x_copies = [
        remote(cot_ref, cotg.at[x], x_send.at[d], x_recv.at[x], {"heads": on_x(d)}) for d in range(1, nx)
    ]
    for copy in x_copies:
        copy.start()
    for side in range(2):
        @pl.when(jnp.logical_not(has[side]))
        def _():
            halo[side] = jnp.zeros(halo.shape[1:], BF16)
            grecv[side] = jnp.zeros(grecv.shape[1:], BF16)
    cotg[x] = cot_ref[...]

    live = live_ref[s]
    counts = []
    for r in range(tiles):
        seen = [jnp.int32(0)] * (tiles + 2)
        for e in range(degree):
            local = slot_ref[nb_ref[s * tiles + r, e]] - s * tiles
            good = jnp.where(mask_ref[s * tiles + r, e] == 1, 1, 0)
            for t in range(tiles):
                seen[t] = seen[t] + jnp.where(local == t, good, 0)
            seen[tiles] = seen[tiles] + jnp.where(local < 0, good, 0)
            seen[tiles + 1] = seen[tiles + 1] + jnp.where(local >= tiles, good, 0)
        counts.append([jnp.where(r < live, n, 0) for n in seen])
    biases = [[jnp.where(n > 0, 0.0, HIDDEN).astype(F32) for n in row] for row in counts]
    counts = [[n.astype(F32) for n in row] for row in counts]

    scale = HD ** (-0.5)
    scaled = q_ref[...].astype(F32) * scale
    lane = lax.broadcasted_iota(jnp.int32, (rows, LANES), 1)
    sub_row = lax.broadcasted_iota(jnp.int32, (LANES, rows), 0)
    q_t = jnp.transpose(scaled)
    for h in range(heads):
        p, i = divmod(h, per)
        mine = jnp.logical_and(sub_row >= i * HD, sub_row < (i + 1) * HD)
        qt[h] = jnp.where(mine, q_t[p * LANES : (p + 1) * LANES, :], 0.0).astype(BF16)
        mine = jnp.logical_and(lane >= i * HD, lane < (i + 1) * HD)
        qm[h] = jnp.where(mine, scaled[:, p * LANES : (p + 1) * LANES], 0.0).astype(BF16)
    own = tiles * TILE
    keys = own + 2 * TILE
    kt[:, 0:own] = turned(k_ref[...]).astype(BF16)
    vt[:, 0:own] = turned(v_ref[...]).astype(BF16)
    for side in range(2):
        @pl.when(has[side])
        def _():
            halo_wait(side).wait_recv()
    for side in range(2):
        at = own + side * TILE
        kt[:, at : at + TILE] = turned(halo[side, 0]).astype(BF16)
        vt[:, at : at + TILE] = turned(halo[side, 1]).astype(BF16)

    for h in range(heads):
        p = h // per
        cols = slice(p * LANES, (p + 1) * LANES)
        blocks = [mm(k_ref[t * TILE : (t + 1) * TILE, cols], qt[h]) for t in range(tiles)]
        blocks += [mm(halo[side, 0, :, cols], qt[h]) for side in range(2)]
        for r in range(tiles):
            span = slice(r * TILE, (r + 1) * TILE)
            parts = [blocks[t][:, span] + biases[r][t] for t in range(tiles + 2)]
            top = functools.reduce(jnp.maximum, [jnp.max(part, axis=0, keepdims=True) for part in parts])
            parts = [jnp.exp(part - top) for part in parts]
            below = sum(jnp.sum(part, axis=0, keepdims=True) * counts[r][t] for t, part in enumerate(parts))
            below = jnp.where(below > 0.0, below, 1.0)
            for t, part in enumerate(parts):
                weight = part * (counts[r][t] / below)
                pf[h, t * TILE : (t + 1) * TILE, span] = weight
                pb[t * TILE : (t + 1) * TILE, h * rows + r * TILE : h * rows + (r + 1) * TILE] = weight.astype(BF16)
        att[h * HD : (h + 1) * HD, :] = mm(
            vt[h * HD : (h + 1) * HD, :], pb[:, h * rows : (h + 1) * rows]
        ).astype(BF16)

    for d in range(1, nx):
        remote(cot_ref, cotg.at[on_x(d)], x_send.at[d], x_recv.at[on_x(d)], {"heads": on_x(d)}).wait_recv()

    def weight_rows(index):
        lines = att[pl.ds(pl.multiple_of(index * half, half), half), :]
        return [mm(lines, cotg[i]) for i in range(nx)]

    p_copies = []
    for d in range(1, ns):
        for i, part in enumerate(weight_rows(on_sub(d))):
            wsend[d - 1, :, i * feats : (i + 1) * feats] = part.astype(BF16)
        copy = remote(wsend.at[d - 1], wrecv.at[d - 1], p_send.at[d], p_recv.at[d], {"sub": on_sub(d)})
        copy.start()
        p_copies.append(copy)
    mine_rows = weight_rows(c)

    dt = sum(mm_nt(w_ref[:, i * feats : (i + 1) * feats], cotg[i]) for i in range(nx)).astype(BF16)
    d_o = turned(dt)
    for h in range(heads):
        p, i = divmod(h, per)
        mine = jnp.logical_and(sub_row >= i * HD, sub_row < (i + 1) * HD)
        dot_t[h] = jnp.where(mine, dt[p * LANES : (p + 1) * LANES, :].astype(F32), 0.0).astype(BF16)
        mine = jnp.logical_and(lane >= i * HD, lane < (i + 1) * HD)
        dom[h] = jnp.where(mine, d_o[:, p * LANES : (p + 1) * LANES], 0.0).astype(BF16)
    product = dt.astype(F32) * att[...].astype(F32)
    deltas = [jnp.sum(product[h * HD : (h + 1) * HD, :], axis=0, keepdims=True) for h in range(heads)]

    for copy in p_copies:
        copy.wait_recv()
    chip = jnp.concatenate(mine_rows, axis=1)
    for d in range(1, ns):
        chip = chip + wrecv[d - 1].astype(F32)
    for j in range(owners):
        zsend[j] = chip[j * piece : (j + 1) * piece, :].astype(BF16)

    def piece_out(j):
        return remote(zsend.at[j], zrecv.at[z], z_send.at[j], z_recv.at[z], {"nodes": jnp.int32(j)})

    for j in range(owners):
        @pl.when(z != j)
        def _():
            piece_out(j).start()

    def score_grads(h, t, values):
        part = mm(values, dot_t[h])
        grad = pf[h, t * TILE : (t + 1) * TILE, :] * (part - deltas[h])
        sb[t * TILE : (t + 1) * TILE, h * rows : (h + 1) * rows] = grad.astype(BF16)

    def key_terms(t, p):
        area = slice(p * per * rows, (p + 1) * per * rows)
        lines = slice(t * TILE, (t + 1) * TILE)
        width = per * rows
        k_part = mm(sb[lines, area], qm[p * per : (p + 1) * per].reshape(width, LANES))
        v_part = mm(pb[lines, area], dom[p * per : (p + 1) * per].reshape(width, LANES))
        return k_part, v_part

    for side in range(2):
        for h in range(heads):
            cols = slice((h // per) * LANES, (h // per + 1) * LANES)
            score_grads(h, tiles + side, halo[side, 1, :, cols])
        for p in range(pairs):
            k_part, v_part = key_terms(tiles + side, p)
            gsend[side, 0, :, p * LANES : (p + 1) * LANES] = k_part.astype(BF16)
            gsend[side, 1, :, p * LANES : (p + 1) * LANES] = v_part.astype(BF16)

        @pl.when(has[side])
        def _():
            grad_copy(side).start()

    factor = total_nodes ** (-0.5)

    def piece_in(j):
        return remote(zsend.at[0], zrecv.at[j], z_send.at[0], z_recv.at[j], {"nodes": z})

    def owner_part():
        acc = zsend[z].astype(F32)
        for d in range(1, nz):
            j = on_z(d)
            piece_in(j).wait_recv()
            acc = acc + zrecv[j].astype(F32)
        ag[c, z] = (acc * factor).astype(BF16)
        for d in range(1, nz):
            remote(ag.at[c, z], ag.at[c, z], a_send.at[d], a_recv.at[z], {"nodes": on_z(d)}).start()
        for d in range(1, ns):
            remote(ag.at[c, z], ag.at[c, z], f_send.at[d - 1, z], f_recv.at[c, z], {"sub": on_sub(d)}).start()

    def forward_part(j):
        remote(ag.at[c, j], ag.at[c, j], a_send.at[0], a_recv.at[j], {"nodes": z}).wait_recv()
        for d in range(1, ns):
            remote(ag.at[c, j], ag.at[c, j], f_send.at[d - 1, j], f_recv.at[c, j], {"sub": on_sub(d)}).start()

    if owners == nz:
        owner_part()
    else:
        pl.when(z < owners)(owner_part)

    for t in range(tiles):
        for h in range(heads):
            cols = slice((h // per) * LANES, (h // per + 1) * LANES)
            score_grads(h, t, v_ref[t * TILE : (t + 1) * TILE, cols])
    own_terms = [[key_terms(t, p) for p in range(pairs)] for t in range(tiles)]
    dq_t = jnp.concatenate(
        [mm(kt[h * HD : (h + 1) * HD, :], sb[:, h * rows : (h + 1) * rows]) for h in range(heads)], axis=0
    )
    dq_ref[...] = (jnp.transpose(dq_t) * scale).astype(BF16)

    for j in range(owners):
        @pl.when(z != j)
        def _():
            forward_part(j)

    for side in range(2):
        @pl.when(has[side])
        def _():
            grad_wait(side).wait_recv()
    for t in range(tiles):
        lines = slice(t * TILE, (t + 1) * TILE)
        gates = [jnp.where(chosen[side] == t, 1.0, 0.0).astype(F32) for side in range(2)]
        for p in range(pairs):
            cols = slice(p * LANES, (p + 1) * LANES)
            for which, out in ((0, dk_ref), (1, dv_ref)):
                value = own_terms[t][p][which]
                for side in range(2):
                    value = value + grecv[side, which, :, cols].astype(F32) * gates[side]
                out[lines, cols] = value.astype(BF16)

    for d in range(1, ns):
        other = on_sub(d)
        for j in range(owners):
            remote(ag.at[c, j], ag.at[other, j], f_send.at[d - 1, j], f_recv.at[other, j], {"sub": other}).wait_recv()
    for i in range(ns):
        for j in range(owners):
            start = i * half + j * piece
            wg_ref[start : start + piece, :] = ag[i, j].astype(F32)

    for side in range(2):
        @pl.when(has[side])
        def _():
            halo_copy(side).wait_send()
            grad_copy(side).wait_send()
    for copy in x_copies:
        copy.wait_send()
    for copy in p_copies:
        copy.wait_send()
    for j in range(owners):
        @pl.when(z != j)
        def _():
            piece_out(j).wait_send()

    def owner_sent():
        for d in range(1, nz):
            remote(ag.at[c, z], ag.at[c, z], a_send.at[d], a_recv.at[z], {"nodes": on_z(d)}).wait_send()

    if owners == nz:
        owner_sent()
    else:
        pl.when(z < owners)(owner_sent)
    for d in range(1, ns):
        for j in range(owners):
            remote(ag.at[c, j], ag.at[c, j], f_send.at[d - 1, j], f_recv.at[c, j], {"sub": on_sub(d)}).wait_send()


def solution(mesh):
    nz, nx, ns = mesh.shape["nodes"], mesh.shape["heads"], mesh.shape["sub"]

    def on_device(
        queries, key_vectors, value_vectors, cotangent, out_weight, neighbours, entry_mask, live_counts, tile_slot
    ):
        rows, feats = queries.shape
        width = out_weight.shape[1]
        tiles, heads = rows // TILE, feats // HD
        keys = (tiles + 2) * TILE
        half = feats // ns
        owners = min(nz, half // 16)
        piece = half // owners
        vmem, smem = pl.BlockSpec(memory_space=pltpu.VMEM), pl.BlockSpec(memory_space=pltpu.SMEM)
        dma = pltpu.SemaphoreType.DMA
        return pl.pallas_call(
            functools.partial(kernel, (nz, nx, ns, owners)),
            out_shape=(
                jax.ShapeDtypeStruct((rows, feats), BF16),
                jax.ShapeDtypeStruct((rows, feats), BF16),
                jax.ShapeDtypeStruct((rows, feats), BF16),
                jax.ShapeDtypeStruct((feats, width), F32),
            ),
            in_specs=[smem] * 4 + [vmem] * 5,
            out_specs=(vmem,) * 4,
            scratch_shapes=[
                pltpu.VMEM((nx, rows, feats), BF16),
                pltpu.VMEM((2, 2, TILE, feats), BF16),
                pltpu.VMEM((2, 2, TILE, feats), BF16),
                pltpu.VMEM((2, 2, TILE, feats), BF16),
                pltpu.VMEM((2, 2, TILE, feats), BF16),
                pltpu.VMEM((heads, LANES, rows), BF16),
                pltpu.VMEM((heads, rows, LANES), BF16),
                pltpu.VMEM((heads, LANES, rows), BF16),
                pltpu.VMEM((heads, rows, LANES), BF16),
                pltpu.VMEM((feats, keys), BF16),
                pltpu.VMEM((feats, keys), BF16),
                pltpu.VMEM((feats, rows), BF16),
                pltpu.VMEM((heads, keys, rows), F32),
                pltpu.VMEM((keys, heads * rows), BF16),
                pltpu.VMEM((keys, heads * rows), BF16),
                pltpu.VMEM((ns - 1, half, width), BF16),
                pltpu.VMEM((ns - 1, half, width), BF16),
                pltpu.VMEM((owners, piece, width), BF16),
                pltpu.VMEM((nz, piece, width), BF16),
                pltpu.VMEM((ns, owners, piece, width), BF16),
                dma((nx,)), dma((nx,)),
                dma((2,)), dma((2,)),
                dma((2,)), dma((2,)),
                dma((ns,)), dma((ns,)),
                dma((owners,)), dma((nz,)),
                dma((nz,)), dma((owners,)),
                dma((ns - 1, owners)), dma((ns, owners)),
            ],
            compiler_params=pltpu.CompilerParams(
                collective_id=0, has_side_effects=True, vmem_limit_bytes=48 * 1024 * 1024
            ),
        )(neighbours, entry_mask, live_counts, tile_slot, queries, key_vectors, value_vectors, cotangent, out_weight)

    part = P(("groups", "nodes", "sub"), "heads")
    return jax.shard_map(
        on_device,
        mesh=mesh,
        in_specs=(
            part, part, part, part, P("heads", None), P("groups", None), P("groups", None), P("groups"), P("groups"),
        ),
        out_specs=(part, part, part, P(("groups", "heads"), None)),
        check_vma=False,
    )
```

```python
import functools

import jax
import jax.numpy as jnp
from jax import lax
from jax.experimental import pallas as pl
from jax.experimental.pallas import tpu as pltpu
from jax.sharding import PartitionSpec as P

HD = 64
TILE = 128
LANES = 128
HIDDEN = -1e30
MESH = pl.DeviceIdType.MESH
F32 = jnp.float32
BF16 = jnp.bfloat16


def mm(a, b):
    return jnp.dot(a, b, preferred_element_type=F32)


def mm_nt(a, b):
    return lax.dot_general(a, b, (((1,), (1,)), ((), ())), preferred_element_type=F32)


def turned(value):
    return jnp.transpose(value.astype(F32))


def kernel(
    sizes,
    nb_hbm, mask_hbm, live_hbm, slot_hbm,
    q_hbm, k_hbm, v_hbm, cot_ref, w_hbm,
    dq_ref, dk_ref, dv_ref, wg_ref,
    nb_ref, mask_ref, live_ref, slot_ref, q_ref, k_ref, v_ref, w_ref, in_sem,
    cotg, hsend, halo, gsend, grecv, qt, qm, dot_t, dom, kt, vt, att, pf, pb, sb, wsend, wrecv, zsend, zrecv, ag,
    x_send, x_recv, h_send, h_recv, g_send, g_recv, p_send, p_recv, z_send, z_recv, a_send, a_recv, f_send, f_recv,
):
    nz, nx, ns, owners = sizes
    rows, feats = q_ref.shape
    tiles = rows // TILE
    heads = feats // HD
    pairs = feats // LANES
    per = LANES // HD
    shards = nz * ns
    half = feats // ns
    piece = half // owners
    degree = nb_ref.shape[1]
    total_nodes = rows * shards
    z, x, c = lax.axis_index("nodes"), lax.axis_index("heads"), lax.axis_index("sub")
    s = z * ns + c
    up, down = jnp.minimum(s + 1, shards - 1), jnp.maximum(s - 1, 0)
    has = (s > 0, s < shards - 1)
    sides = (down, up)

    def at_shard(index):
        return {"nodes": lax.div(index, ns), "sub": lax.rem(index, ns)}

    def on_x(d):
        return lax.rem(x + d, nx)

    def on_z(d):
        return lax.rem(z + d, nz)

    def on_sub(d):
        return lax.rem(c + d, ns)

    cross = (jnp.logical_and(c == 0, z > 0), jnp.logical_and(c == ns - 1, z < nz - 1))

    def load(index):
        return pltpu.make_async_copy(*incoming[index], in_sem.at[index])

    incoming = (
        (nb_hbm, nb_ref), (slot_hbm, slot_ref), (k_hbm, k_ref), (v_hbm, v_ref), (mask_hbm, mask_ref),
        (live_hbm, live_ref), (q_hbm, q_ref), (cot_ref, cotg.at[x]), (w_hbm, w_ref),
    )
    for i in range(len(incoming)):
        load(i).start()
    barrier = pltpu.get_barrier_semaphore()

    def greet(device):
        pl.semaphore_signal(barrier, inc=1, device_id=device, device_id_type=MESH)

    for d in range(1, nx):
        greet({"heads": on_x(d)})
    for d in range(1, ns):
        greet({"sub": on_sub(d)})
    for side in range(2):
        @pl.when(cross[side])
        def _():
            greet(at_shard(sides[side]))
    for d in range(1, nz):
        greet({"nodes": on_z(d)})

    load(0).wait()
    load(1).wait()
    chosen = []
    for side in range(2):
        pick = jnp.int32(0)
        for r in range(tiles):
            for e in range(degree):
                slot = slot_ref[nb_ref[sides[side] * tiles + r, e]]
                local = slot - s * tiles
                inside = jnp.logical_and(local >= 0, local < tiles)
                pick = jnp.where(inside, local, pick)
        chosen.append(pick)
    load(2).wait()
    load(3).wait()
    for side in range(2):
        kk, vv = k_ref[0:TILE, :], v_ref[0:TILE, :]
        for t in range(1, tiles):
            here = chosen[side] == t
            kk = jnp.where(here, k_ref[t * TILE : (t + 1) * TILE, :], kk)
            vv = jnp.where(here, v_ref[t * TILE : (t + 1) * TILE, :], vv)
        hsend[side, 0] = kk
        hsend[side, 1] = vv

    extra = jnp.where(jnp.logical_or(cross[0], cross[1]), 1, 0)
    pl.semaphore_wait(barrier, nx - 1 + ns - 1 + nz - 1 + extra)

    def remote(src, dst, send, recv, device):
        return pltpu.make_async_remote_copy(
            src_ref=src, dst_ref=dst, send_sem=send, recv_sem=recv, device_id=device, device_id_type=MESH
        )

    def halo_copy(side):
        return remote(hsend.at[side], halo.at[1 - side], h_send.at[side], h_recv.at[1 - side], at_shard(sides[side]))

    def halo_wait(side):
        return remote(hsend.at[side], halo.at[side], h_send.at[side], h_recv.at[side], at_shard(sides[side]))

    def grad_copy(side):
        return remote(gsend.at[side], grecv.at[1 - side], g_send.at[side], g_recv.at[1 - side], at_shard(sides[side]))

    def grad_wait(side):
        return remote(gsend.at[side], grecv.at[side], g_send.at[side], g_recv.at[side], at_shard(sides[side]))

    for side in range(2):
        @pl.when(has[side])
        def _():
            halo_copy(side).start()

    x_copies = [
        remote(cot_ref, cotg.at[x], x_send.at[d], x_recv.at[x], {"heads": on_x(d)}) for d in range(1, nx)
    ]
    for copy in x_copies:
        copy.start()
    for side in range(2):
        @pl.when(jnp.logical_not(has[side]))
        def _():
            halo[side] = jnp.zeros(halo.shape[1:], BF16)
            grecv[side] = jnp.zeros(grecv.shape[1:], BF16)

    load(4).wait()
    load(5).wait()
    live = live_ref[s]
    counts = []
    for r in range(tiles):
        seen = [jnp.int32(0)] * (tiles + 2)
        for e in range(degree):
            local = slot_ref[nb_ref[s * tiles + r, e]] - s * tiles
            good = jnp.where(mask_ref[s * tiles + r, e] == 1, 1, 0)
            for t in range(tiles):
                seen[t] = seen[t] + jnp.where(local == t, good, 0)
            seen[tiles] = seen[tiles] + jnp.where(local < 0, good, 0)
            seen[tiles + 1] = seen[tiles + 1] + jnp.where(local >= tiles, good, 0)
        counts.append([jnp.where(r < live, n, 0) for n in seen])
    biases = [[jnp.where(n > 0, 0.0, HIDDEN).astype(F32) for n in row] for row in counts]
    counts = [[n.astype(F32) for n in row] for row in counts]

    scale = HD ** (-0.5)
    load(6).wait()
    scaled = q_ref[...].astype(F32) * scale
    lane = lax.broadcasted_iota(jnp.int32, (rows, LANES), 1)
    sub_row = lax.broadcasted_iota(jnp.int32, (LANES, rows), 0)
    q_t = jnp.transpose(scaled)
    for h in range(heads):
        p, i = divmod(h, per)
        mine = jnp.logical_and(sub_row >= i * HD, sub_row < (i + 1) * HD)
        qt[h] = jnp.where(mine, q_t[p * LANES : (p + 1) * LANES, :], 0.0).astype(BF16)
        mine = jnp.logical_and(lane >= i * HD, lane < (i + 1) * HD)
        qm[h] = jnp.where(mine, scaled[:, p * LANES : (p + 1) * LANES], 0.0).astype(BF16)
    own = tiles * TILE
    keys = own + 2 * TILE
    kt[:, 0:own] = turned(k_ref[...]).astype(BF16)
    vt[:, 0:own] = turned(v_ref[...]).astype(BF16)
    for side in range(2):
        @pl.when(has[side])
        def _():
            halo_wait(side).wait_recv()
    for side in range(2):
        at = own + side * TILE
        kt[:, at : at + TILE] = turned(halo[side, 0]).astype(BF16)
        vt[:, at : at + TILE] = turned(halo[side, 1]).astype(BF16)

    for h in range(heads):
        p = h // per
        cols = slice(p * LANES, (p + 1) * LANES)
        blocks = [mm(k_ref[t * TILE : (t + 1) * TILE, cols], qt[h]) for t in range(tiles)]
        blocks += [mm(halo[side, 0, :, cols], qt[h]) for side in range(2)]
        for r in range(tiles):
            span = slice(r * TILE, (r + 1) * TILE)
            parts = [blocks[t][:, span] + biases[r][t] for t in range(tiles + 2)]
            top = functools.reduce(jnp.maximum, [jnp.max(part, axis=0, keepdims=True) for part in parts])
            parts = [jnp.exp(part - top) for part in parts]
            below = sum(jnp.sum(part, axis=0, keepdims=True) * counts[r][t] for t, part in enumerate(parts))
            below = jnp.where(below > 0.0, below, 1.0)
            for t, part in enumerate(parts):
                weight = part * (counts[r][t] / below)
                pf[h, t * TILE : (t + 1) * TILE, span] = weight
                pb[t * TILE : (t + 1) * TILE, h * rows + r * TILE : h * rows + (r + 1) * TILE] = weight.astype(BF16)
        att[h * HD : (h + 1) * HD, :] = mm(
            vt[h * HD : (h + 1) * HD, :], pb[:, h * rows : (h + 1) * rows]
        ).astype(BF16)

    load(7).wait()
    load(8).wait()
    for d in range(1, nx):
        remote(cot_ref, cotg.at[on_x(d)], x_send.at[d], x_recv.at[on_x(d)], {"heads": on_x(d)}).wait_recv()

    def weight_rows(index):
        lines = att[pl.ds(pl.multiple_of(index * half, half), half), :]
        return [mm(lines, cotg[i]) for i in range(nx)]

    p_copies = []
    for d in range(1, ns):
        for i, part in enumerate(weight_rows(on_sub(d))):
            wsend[d - 1, :, i * feats : (i + 1) * feats] = part.astype(BF16)
        copy = remote(wsend.at[d - 1], wrecv.at[d - 1], p_send.at[d], p_recv.at[d], {"sub": on_sub(d)})
        copy.start()
        p_copies.append(copy)
    mine_rows = weight_rows(c)

    dt = sum(mm_nt(w_ref[:, i * feats : (i + 1) * feats], cotg[i]) for i in range(nx)).astype(BF16)
    d_o = turned(dt)
    for h in range(heads):
        p, i = divmod(h, per)
        mine = jnp.logical_and(sub_row >= i * HD, sub_row < (i + 1) * HD)
        dot_t[h] = jnp.where(mine, dt[p * LANES : (p + 1) * LANES, :].astype(F32), 0.0).astype(BF16)
        mine = jnp.logical_and(lane >= i * HD, lane < (i + 1) * HD)
        dom[h] = jnp.where(mine, d_o[:, p * LANES : (p + 1) * LANES], 0.0).astype(BF16)
    product = dt.astype(F32) * att[...].astype(F32)
    deltas = [jnp.sum(product[h * HD : (h + 1) * HD, :], axis=0, keepdims=True) for h in range(heads)]

    for copy in p_copies:
        copy.wait_recv()
    chip = jnp.concatenate(mine_rows, axis=1)
    for d in range(1, ns):
        chip = chip + wrecv[d - 1].astype(F32)
    for j in range(owners):
        zsend[j] = chip[j * piece : (j + 1) * piece, :].astype(BF16)

    def piece_out(j):
        return remote(zsend.at[j], zrecv.at[z], z_send.at[j], z_recv.at[z], {"nodes": jnp.int32(j)})

    for j in range(owners):
        @pl.when(z != j)
        def _():
            piece_out(j).start()

    def score_grads(h, t, values):
        part = mm(values, dot_t[h])
        grad = pf[h, t * TILE : (t + 1) * TILE, :] * (part - deltas[h])
        sb[t * TILE : (t + 1) * TILE, h * rows : (h + 1) * rows] = grad.astype(BF16)

    def key_terms(t, p):
        area = slice(p * per * rows, (p + 1) * per * rows)
        lines = slice(t * TILE, (t + 1) * TILE)
        width = per * rows
        k_part = mm(sb[lines, area], qm[p * per : (p + 1) * per].reshape(width, LANES))
        v_part = mm(pb[lines, area], dom[p * per : (p + 1) * per].reshape(width, LANES))
        return k_part, v_part

    for side in range(2):
        for h in range(heads):
            cols = slice((h // per) * LANES, (h // per + 1) * LANES)
            score_grads(h, tiles + side, halo[side, 1, :, cols])
        for p in range(pairs):
            k_part, v_part = key_terms(tiles + side, p)
            gsend[side, 0, :, p * LANES : (p + 1) * LANES] = k_part.astype(BF16)
            gsend[side, 1, :, p * LANES : (p + 1) * LANES] = v_part.astype(BF16)

        @pl.when(has[side])
        def _():
            grad_copy(side).start()

    factor = total_nodes ** (-0.5)

    def piece_in(j):
        return remote(zsend.at[0], zrecv.at[j], z_send.at[0], z_recv.at[j], {"nodes": z})

    def owner_part():
        acc = zsend[z].astype(F32)
        for d in range(1, nz):
            j = on_z(d)
            piece_in(j).wait_recv()
            acc = acc + zrecv[j].astype(F32)
        ag[c, z] = (acc * factor).astype(BF16)
        for d in range(1, nz):
            remote(ag.at[c, z], ag.at[c, z], a_send.at[d], a_recv.at[z], {"nodes": on_z(d)}).start()
        for d in range(1, ns):
            remote(ag.at[c, z], ag.at[c, z], f_send.at[d - 1, z], f_recv.at[c, z], {"sub": on_sub(d)}).start()

    def forward_part(j):
        remote(ag.at[c, j], ag.at[c, j], a_send.at[0], a_recv.at[j], {"nodes": z}).wait_recv()
        for d in range(1, ns):
            remote(ag.at[c, j], ag.at[c, j], f_send.at[d - 1, j], f_recv.at[c, j], {"sub": on_sub(d)}).start()

    if owners == nz:
        owner_part()
    else:
        pl.when(z < owners)(owner_part)

    for t in range(tiles):
        for h in range(heads):
            cols = slice((h // per) * LANES, (h // per + 1) * LANES)
            score_grads(h, t, v_ref[t * TILE : (t + 1) * TILE, cols])
    own_terms = [[key_terms(t, p) for p in range(pairs)] for t in range(tiles)]
    dq_t = jnp.concatenate(
        [mm(kt[h * HD : (h + 1) * HD, :], sb[:, h * rows : (h + 1) * rows]) for h in range(heads)], axis=0
    )
    dq_ref[...] = (jnp.transpose(dq_t) * scale).astype(BF16)

    for j in range(owners):
        @pl.when(z != j)
        def _():
            forward_part(j)

    for side in range(2):
        @pl.when(has[side])
        def _():
            grad_wait(side).wait_recv()
    for t in range(tiles):
        lines = slice(t * TILE, (t + 1) * TILE)
        gates = [jnp.where(chosen[side] == t, 1.0, 0.0).astype(F32) for side in range(2)]
        for p in range(pairs):
            cols = slice(p * LANES, (p + 1) * LANES)
            for which, out in ((0, dk_ref), (1, dv_ref)):
                value = own_terms[t][p][which]
                for side in range(2):
                    value = value + grecv[side, which, :, cols].astype(F32) * gates[side]
                out[lines, cols] = value.astype(BF16)

    for d in range(1, ns):
        other = on_sub(d)
        for j in range(owners):
            remote(ag.at[c, j], ag.at[other, j], f_send.at[d - 1, j], f_recv.at[other, j], {"sub": other}).wait_recv()
    for i in range(ns):
        for j in range(owners):
            start = i * half + j * piece
            wg_ref[start : start + piece, :] = ag[i, j]

    for side in range(2):
        @pl.when(has[side])
        def _():
            halo_copy(side).wait_send()
            grad_copy(side).wait_send()
    for copy in x_copies:
        copy.wait_send()
    for copy in p_copies:
        copy.wait_send()
    for j in range(owners):
        @pl.when(z != j)
        def _():
            piece_out(j).wait_send()

    def owner_sent():
        for d in range(1, nz):
            remote(ag.at[c, z], ag.at[c, z], a_send.at[d], a_recv.at[z], {"nodes": on_z(d)}).wait_send()

    if owners == nz:
        owner_sent()
    else:
        pl.when(z < owners)(owner_sent)
    for d in range(1, ns):
        for j in range(owners):
            remote(ag.at[c, j], ag.at[c, j], f_send.at[d - 1, j], f_recv.at[c, j], {"sub": on_sub(d)}).wait_send()


def deliver(dq_ref, dk_ref, dv_ref, wg_ref, dq_out, dk_out, dv_out, wg_out, wide, sem):
    copies = [
        pltpu.make_async_copy(dq_ref, dq_out, sem.at[0]),
        pltpu.make_async_copy(dk_ref, dk_out, sem.at[1]),
        pltpu.make_async_copy(dv_ref, dv_out, sem.at[2]),
        pltpu.make_async_copy(wide, wg_out, sem.at[3]),
    ]
    for copy in copies[:3]:
        copy.start()
    wide[...] = wg_ref[...].astype(F32)
    copies[3].start()
    for copy in copies:
        copy.wait()


def solution(mesh):
    nz, nx, ns = mesh.shape["nodes"], mesh.shape["heads"], mesh.shape["sub"]

    def on_device(
        queries, key_vectors, value_vectors, cotangent, out_weight, neighbours, entry_mask, live_counts, tile_slot
    ):
        rows, feats = queries.shape
        width = out_weight.shape[1]
        tiles, heads = rows // TILE, feats // HD
        keys = (tiles + 2) * TILE
        half = feats // ns
        owners = min(nz, half // 16)
        piece = half // owners
        vmem, hbm = pl.BlockSpec(memory_space=pltpu.VMEM), pl.BlockSpec(memory_space=pltpu.HBM)
        dma = pltpu.SemaphoreType.DMA
        partial = pl.pallas_call(
            functools.partial(kernel, (nz, nx, ns, owners)),
            out_shape=(
                jax.ShapeDtypeStruct((rows, feats), BF16),
                jax.ShapeDtypeStruct((rows, feats), BF16),
                jax.ShapeDtypeStruct((rows, feats), BF16),
                jax.ShapeDtypeStruct((feats, width), BF16),
            ),
            in_specs=[hbm] * 9,
            out_specs=(vmem,) * 4,
            scratch_shapes=[
                pltpu.SMEM(neighbours.shape, jnp.int32),
                pltpu.SMEM(entry_mask.shape, jnp.int32),
                pltpu.SMEM(live_counts.shape, jnp.int32),
                pltpu.SMEM(tile_slot.shape, jnp.int32),
                pltpu.VMEM((rows, feats), BF16),
                pltpu.VMEM((rows, feats), BF16),
                pltpu.VMEM((rows, feats), BF16),
                pltpu.VMEM((feats, width), BF16),
                dma((9,)),
                pltpu.VMEM((nx, rows, feats), BF16),
                pltpu.VMEM((2, 2, TILE, feats), BF16),
                pltpu.VMEM((2, 2, TILE, feats), BF16),
                pltpu.VMEM((2, 2, TILE, feats), BF16),
                pltpu.VMEM((2, 2, TILE, feats), BF16),
                pltpu.VMEM((heads, LANES, rows), BF16),
                pltpu.VMEM((heads, rows, LANES), BF16),
                pltpu.VMEM((heads, LANES, rows), BF16),
                pltpu.VMEM((heads, rows, LANES), BF16),
                pltpu.VMEM((feats, keys), BF16),
                pltpu.VMEM((feats, keys), BF16),
                pltpu.VMEM((feats, rows), BF16),
                pltpu.VMEM((heads, keys, rows), F32),
                pltpu.VMEM((keys, heads * rows), BF16),
                pltpu.VMEM((keys, heads * rows), BF16),
                pltpu.VMEM((ns - 1, half, width), BF16),
                pltpu.VMEM((ns - 1, half, width), BF16),
                pltpu.VMEM((owners, piece, width), BF16),
                pltpu.VMEM((nz, piece, width), BF16),
                pltpu.VMEM((ns, owners, piece, width), BF16),
                dma((nx,)), dma((nx,)),
                dma((2,)), dma((2,)),
                dma((2,)), dma((2,)),
                dma((ns,)), dma((ns,)),
                dma((owners,)), dma((nz,)),
                dma((nz,)), dma((owners,)),
                dma((ns - 1, owners)), dma((ns, owners)),
            ],
            compiler_params=pltpu.CompilerParams(
                collective_id=0, has_side_effects=True, vmem_limit_bytes=48 * 1024 * 1024
            ),
        )(
            *(
                pltpu.with_memory_space_constraint(array, pltpu.HBM)
                for array in (
                    neighbours, entry_mask, live_counts, tile_slot,
                    queries, key_vectors, value_vectors, cotangent, out_weight,
                )
            )
        )
        return pl.pallas_call(
            deliver,
            out_shape=(
                jax.ShapeDtypeStruct((rows, feats), BF16),
                jax.ShapeDtypeStruct((rows, feats), BF16),
                jax.ShapeDtypeStruct((rows, feats), BF16),
                jax.ShapeDtypeStruct((feats, width), F32),
            ),
            in_specs=[vmem] * 4,
            out_specs=(hbm,) * 4,
            scratch_shapes=[pltpu.VMEM((feats, width), F32), dma((4,))],
            compiler_params=pltpu.CompilerParams(vmem_limit_bytes=4 * 1024 * 1024),
        )(*partial)

    part = P(("groups", "nodes", "sub"), "heads")
    return jax.shard_map(
        on_device,
        mesh=mesh,
        in_specs=(
            part, part, part, part, P("heads", None), P("groups", None), P("groups", None), P("groups"), P("groups"),
        ),
        out_specs=(part, part, part, P(("groups", "heads"), None)),
        check_vma=False,
    )
```

```python
import functools

import jax
import jax.numpy as jnp
from jax import lax
from jax.experimental import pallas as pl
from jax.experimental.pallas import tpu as pltpu
from jax.sharding import PartitionSpec as P

HD = 64
TILE = 128
LANES = 128
HIDDEN = -1e30
MESH = pl.DeviceIdType.MESH
F32 = jnp.float32
BF16 = jnp.bfloat16


def mm(a, b):
    return jnp.dot(a, b, preferred_element_type=F32)


def mm_nt(a, b):
    return lax.dot_general(a, b, (((1,), (1,)), ((), ())), preferred_element_type=F32)


def turned(value):
    return jnp.transpose(value.astype(F32))


def kernel(
    sizes,
    nb_hbm, mask_hbm, live_hbm, slot_hbm,
    q_hbm, k_hbm, v_hbm, cot_ref, w_hbm,
    dq_ref, dk_ref, dv_ref, wg_ref,
    nb_ref, mask_ref, live_ref, slot_ref, q_ref, k_ref, v_ref, w_ref, in_sem,
    cotg, hsend, halo, gsend, grecv, qt, qm, dot_t, dom, kt, vt, att, pf, pb, sb, wsend, wrecv, zsend, zrecv, ag, stat,
    x_send, x_recv, h_send, h_recv, g_send, g_recv, p_send, p_recv, z_send, z_recv, a_send, a_recv, f_send, f_recv,
):
    nz, nx, ns, owners = sizes
    rows, feats = q_ref.shape
    tiles = rows // TILE
    heads = feats // HD
    pairs = feats // LANES
    per = LANES // HD
    shards = nz * ns
    half = feats // ns
    piece = half // owners
    degree = nb_ref.shape[1]
    total_nodes = rows * shards
    z, x, c = lax.axis_index("nodes"), lax.axis_index("heads"), lax.axis_index("sub")
    s = z * ns + c
    up, down = jnp.minimum(s + 1, shards - 1), jnp.maximum(s - 1, 0)
    has = (s > 0, s < shards - 1)
    sides = (down, up)

    def at_shard(index):
        return {"nodes": lax.div(index, ns), "sub": lax.rem(index, ns)}

    def on_x(d):
        return lax.rem(x + d, nx)

    def on_z(d):
        return lax.rem(z + d, nz)

    def on_sub(d):
        return lax.rem(c + d, ns)

    cross = (jnp.logical_and(c == 0, z > 0), jnp.logical_and(c == ns - 1, z < nz - 1))

    def load(index):
        return pltpu.make_async_copy(*incoming[index], in_sem.at[index])

    incoming = (
        (nb_hbm, nb_ref), (slot_hbm, slot_ref), (k_hbm, k_ref), (v_hbm, v_ref), (mask_hbm, mask_ref),
        (live_hbm, live_ref), (q_hbm, q_ref), (cot_ref, cotg.at[x]), (w_hbm, w_ref),
    )
    for i in range(len(incoming)):
        load(i).start()
    barrier = pltpu.get_barrier_semaphore()

    def greet(device):
        pl.semaphore_signal(barrier, inc=1, device_id=device, device_id_type=MESH)

    for d in range(1, nx):
        greet({"heads": on_x(d)})
    for d in range(1, ns):
        greet({"sub": on_sub(d)})
    for side in range(2):
        @pl.when(cross[side])
        def _():
            greet(at_shard(sides[side]))
    for d in range(1, nz):
        greet({"nodes": on_z(d)})

    load(0).wait()
    load(1).wait()
    chosen = []
    for side in range(2):
        pick = jnp.int32(0)
        for r in range(tiles):
            for e in range(degree):
                slot = slot_ref[nb_ref[sides[side] * tiles + r, e]]
                local = slot - s * tiles
                inside = jnp.logical_and(local >= 0, local < tiles)
                pick = jnp.where(inside, local, pick)
        chosen.append(pick)
    load(2).wait()
    load(3).wait()
    for side in range(2):
        kk, vv = k_ref[0:TILE, :], v_ref[0:TILE, :]
        for t in range(1, tiles):
            here = chosen[side] == t
            kk = jnp.where(here, k_ref[t * TILE : (t + 1) * TILE, :], kk)
            vv = jnp.where(here, v_ref[t * TILE : (t + 1) * TILE, :], vv)
        hsend[side, 0] = kk
        hsend[side, 1] = vv

    extra = jnp.where(jnp.logical_or(cross[0], cross[1]), 1, 0)
    pl.semaphore_wait(barrier, nx - 1 + ns - 1 + nz - 1 + extra)

    def remote(src, dst, send, recv, device):
        return pltpu.make_async_remote_copy(
            src_ref=src, dst_ref=dst, send_sem=send, recv_sem=recv, device_id=device, device_id_type=MESH
        )

    def halo_copy(side):
        return remote(hsend.at[side], halo.at[1 - side], h_send.at[side], h_recv.at[1 - side], at_shard(sides[side]))

    def halo_wait(side):
        return remote(hsend.at[side], halo.at[side], h_send.at[side], h_recv.at[side], at_shard(sides[side]))

    def grad_copy(side):
        return remote(gsend.at[side], grecv.at[1 - side], g_send.at[side], g_recv.at[1 - side], at_shard(sides[side]))

    def grad_wait(side):
        return remote(gsend.at[side], grecv.at[side], g_send.at[side], g_recv.at[side], at_shard(sides[side]))

    for side in range(2):
        @pl.when(has[side])
        def _():
            halo_copy(side).start()

    x_copies = [
        remote(cot_ref, cotg.at[x], x_send.at[d], x_recv.at[x], {"heads": on_x(d)}) for d in range(1, nx)
    ]
    for copy in x_copies:
        copy.start()
    for side in range(2):
        @pl.when(jnp.logical_not(has[side]))
        def _():
            halo[side] = jnp.zeros(halo.shape[1:], BF16)
            grecv[side] = jnp.zeros(grecv.shape[1:], BF16)

    load(4).wait()
    load(5).wait()
    live = live_ref[s]
    counts = []
    for r in range(tiles):
        seen = [jnp.int32(0)] * (tiles + 2)
        for e in range(degree):
            local = slot_ref[nb_ref[s * tiles + r, e]] - s * tiles
            good = jnp.where(mask_ref[s * tiles + r, e] == 1, 1, 0)
            for t in range(tiles):
                seen[t] = seen[t] + jnp.where(local == t, good, 0)
            seen[tiles] = seen[tiles] + jnp.where(local < 0, good, 0)
            seen[tiles + 1] = seen[tiles + 1] + jnp.where(local >= tiles, good, 0)
        counts.append([jnp.where(r < live, n, 0) for n in seen])
    biases = [[jnp.where(n > 0, 0.0, HIDDEN).astype(F32) for n in row] for row in counts]
    counts = [[n.astype(F32) for n in row] for row in counts]

    scale = HD ** (-0.5)
    load(6).wait()
    scaled = q_ref[...].astype(F32) * scale
    lane = lax.broadcasted_iota(jnp.int32, (rows, LANES), 1)
    sub_row = lax.broadcasted_iota(jnp.int32, (LANES, rows), 0)
    q_t = jnp.transpose(scaled)
    for h in range(heads):
        p, i = divmod(h, per)
        mine = jnp.logical_and(sub_row >= i * HD, sub_row < (i + 1) * HD)
        qt[h] = jnp.where(mine, q_t[p * LANES : (p + 1) * LANES, :], 0.0).astype(BF16)
        mine = jnp.logical_and(lane >= i * HD, lane < (i + 1) * HD)
        qm[h] = jnp.where(mine, scaled[:, p * LANES : (p + 1) * LANES], 0.0).astype(BF16)
    own = tiles * TILE
    keys = own + 2 * TILE
    kt[:, 0:own] = turned(k_ref[...]).astype(BF16)
    vt[:, 0:own] = turned(v_ref[...]).astype(BF16)
    for h in range(heads):
        cols = slice((h // per) * LANES, (h // per + 1) * LANES)
        blocks = [mm(k_ref[t * TILE : (t + 1) * TILE, cols], qt[h]) for t in range(tiles)]
        for r in range(tiles):
            span = slice(r * TILE, (r + 1) * TILE)
            parts = [blocks[t][:, span] + biases[r][t] for t in range(tiles)]
            top = functools.reduce(jnp.maximum, [jnp.max(part, axis=0, keepdims=True) for part in parts])
            parts = [jnp.exp(part - top) for part in parts]
            stat[0, h, :, span] = top
            stat[1, h, :, span] = sum(
                jnp.sum(part, axis=0, keepdims=True) * counts[r][t] for t, part in enumerate(parts)
            )
            for t, part in enumerate(parts):
                pf[h, t * TILE : (t + 1) * TILE, span] = part
    for side in range(2):
        @pl.when(has[side])
        def _():
            halo_wait(side).wait_recv()
    for side in range(2):
        at = own + side * TILE
        kt[:, at : at + TILE] = turned(halo[side, 0]).astype(BF16)
        vt[:, at : at + TILE] = turned(halo[side, 1]).astype(BF16)

    def attend(h):
        cols = pl.ds(pl.multiple_of(lax.div(h, per) * LANES, LANES), LANES)
        blocks = [mm(halo[side, 0, :, cols], qt[h]) for side in range(2)]
        for r in range(tiles):
            span = slice(r * TILE, (r + 1) * TILE)
            into = pl.ds(pl.multiple_of(h * rows + r * TILE, TILE), TILE)
            parts = [blocks[side][:, span] + biases[r][tiles + side] for side in range(2)]
            before = stat[0, h, :, span]
            top = functools.reduce(jnp.maximum, [jnp.max(part, axis=0, keepdims=True) for part in parts], before)
            parts = [jnp.exp(part - top) for part in parts]
            shrink = jnp.exp(before - top)
            below = stat[1, h, :, span] * shrink + sum(
                jnp.sum(part, axis=0, keepdims=True) * counts[r][tiles + side] for side, part in enumerate(parts)
            )
            over = 1.0 / jnp.where(below > 0.0, below, 1.0)
            for t in range(tiles + 2):
                lines = slice(t * TILE, (t + 1) * TILE)
                if t < tiles:
                    weight = pf[h, lines, span] * (counts[r][t] * shrink * over)
                else:
                    weight = parts[t - tiles] * (counts[r][t] * over)
                pf[h, lines, span] = weight
                pb[lines, into] = weight.astype(BF16)
        lines = pl.ds(pl.multiple_of(h * HD, HD), HD)
        att[lines, :] = mm(vt[lines, :], pb[:, pl.ds(pl.multiple_of(h * rows, rows), rows)]).astype(BF16)

    def weight_rows(index, i):
        return mm(att[pl.ds(pl.multiple_of(index * half, half), half), :], cotg[on_x(i)])

    def pair_copy(d, i):
        return remote(
            wsend.at[d - 1, i], wrecv.at[d - 1, i], p_send.at[d - 1, i], p_recv.at[d - 1, i], {"sub": on_sub(d)}
        )

    def pair_start(d, i):
        wsend[d - 1, i] = weight_rows(on_sub(d), i).astype(BF16)
        pair_copy(d, i).start()

    here = heads // ns
    load(7).wait()
    for d in range(1, ns):
        for i in range(here):
            attend(on_sub(d) * here + i)
        pair_start(d, 0)
    for i in range(here):
        attend(c * here + i)
    mine_rows = [weight_rows(c, 0)]
    load(8).wait()
    for d in range(1, nx):
        remote(cot_ref, cotg.at[on_x(d)], x_send.at[d], x_recv.at[on_x(d)], {"heads": on_x(d)}).wait_recv()
    for i in range(1, nx):
        for d in range(1, ns):
            pair_start(d, i)
        mine_rows.append(weight_rows(c, i))

    def piece_out(i, j):
        return remote(zsend.at[i, j], zrecv.at[i, z], z_send.at[i, j], z_recv.at[i, z], {"nodes": jnp.int32(j)})

    def spread(i):
        for d in range(1, ns):
            pair_copy(d, i).wait_recv()
        chip = mine_rows[i]
        for d in range(1, ns):
            chip = chip + wrecv[d - 1, i].astype(F32)
        for j in range(owners):
            zsend[i, j] = chip[j * piece : (j + 1) * piece, :].astype(BF16)
        for j in range(owners):
            @pl.when(z != j)
            def _():
                piece_out(i, j).start()

    spread(0)
    dt = sum(mm_nt(w_ref[:, i * feats : (i + 1) * feats], cotg[i]) for i in range(nx)).astype(BF16)
    d_o = turned(dt)
    for h in range(heads):
        p, i = divmod(h, per)
        mine = jnp.logical_and(sub_row >= i * HD, sub_row < (i + 1) * HD)
        dot_t[h] = jnp.where(mine, dt[p * LANES : (p + 1) * LANES, :].astype(F32), 0.0).astype(BF16)
        mine = jnp.logical_and(lane >= i * HD, lane < (i + 1) * HD)
        dom[h] = jnp.where(mine, d_o[:, p * LANES : (p + 1) * LANES], 0.0).astype(BF16)
    product = dt.astype(F32) * att[...].astype(F32)
    deltas = [jnp.sum(product[h * HD : (h + 1) * HD, :], axis=0, keepdims=True) for h in range(heads)]
    for i in range(1, nx):
        spread(i)
    def score_grads(h, t, values):
        part = mm(values, dot_t[h])
        grad = pf[h, t * TILE : (t + 1) * TILE, :] * (part - deltas[h])
        sb[t * TILE : (t + 1) * TILE, h * rows : (h + 1) * rows] = grad.astype(BF16)

    def key_terms(t, p):
        area = slice(p * per * rows, (p + 1) * per * rows)
        lines = slice(t * TILE, (t + 1) * TILE)
        width = per * rows
        k_part = mm(sb[lines, area], qm[p * per : (p + 1) * per].reshape(width, LANES))
        v_part = mm(pb[lines, area], dom[p * per : (p + 1) * per].reshape(width, LANES))
        return k_part, v_part

    for side in range(2):
        for h in range(heads):
            cols = slice((h // per) * LANES, (h // per + 1) * LANES)
            score_grads(h, tiles + side, halo[side, 1, :, cols])
        for p in range(pairs):
            k_part, v_part = key_terms(tiles + side, p)
            gsend[side, 0, :, p * LANES : (p + 1) * LANES] = k_part.astype(BF16)
            gsend[side, 1, :, p * LANES : (p + 1) * LANES] = v_part.astype(BF16)

        @pl.when(has[side])
        def _():
            grad_copy(side).start()

    factor = total_nodes ** (-0.5)

    def piece_in(i, j):
        return remote(zsend.at[i, 0], zrecv.at[i, j], z_send.at[i, 0], z_recv.at[i, j], {"nodes": z})

    def to_owner_peer(i, d):
        return remote(ag.at[i, c, z], ag.at[i, c, z], a_send.at[i, d], a_recv.at[i, z], {"nodes": on_z(d)})

    def to_core(i, j, d):
        return remote(ag.at[i, c, j], ag.at[i, c, j], f_send.at[i, d - 1, j], f_recv.at[i, c, j], {"sub": on_sub(d)})

    def owner_part():
        for i in range(nx):
            acc = zsend[i, z].astype(F32)
            for d in range(1, nz):
                j = on_z(d)
                piece_in(i, j).wait_recv()
                acc = acc + zrecv[i, j].astype(F32)
            ag[i, c, z] = (acc * factor).astype(BF16)
            for d in range(1, nz):
                to_owner_peer(i, d).start()
            for d in range(1, ns):
                to_core(i, z, d).start()

    def forward_part(i, j):
        remote(ag.at[i, c, j], ag.at[i, c, j], a_send.at[i, 0], a_recv.at[i, j], {"nodes": z}).wait_recv()
        for d in range(1, ns):
            to_core(i, j, d).start()

    if owners == nz:
        owner_part()
    else:
        pl.when(z < owners)(owner_part)

    for t in range(tiles):
        for h in range(heads):
            cols = slice((h // per) * LANES, (h // per + 1) * LANES)
            score_grads(h, t, v_ref[t * TILE : (t + 1) * TILE, cols])
    own_terms = [[key_terms(t, p) for p in range(pairs)] for t in range(tiles)]
    dq_t = jnp.concatenate(
        [mm(kt[h * HD : (h + 1) * HD, :], sb[:, h * rows : (h + 1) * rows]) for h in range(heads)], axis=0
    )
    dq_ref[...] = (jnp.transpose(dq_t) * scale).astype(BF16)


    for side in range(2):
        @pl.when(has[side])
        def _():
            grad_wait(side).wait_recv()
    for t in range(tiles):
        lines = slice(t * TILE, (t + 1) * TILE)
        gates = [jnp.where(chosen[side] == t, 1.0, 0.0).astype(F32) for side in range(2)]
        for p in range(pairs):
            cols = slice(p * LANES, (p + 1) * LANES)
            for which, out in ((0, dk_ref), (1, dv_ref)):
                value = own_terms[t][p][which]
                for side in range(2):
                    value = value + grecv[side, which, :, cols].astype(F32) * gates[side]
                out[lines, cols] = value.astype(BF16)

    for i in range(nx):
        for j in range(owners):
            @pl.when(z != j)
            def _():
                forward_part(i, j)
    for i in range(nx):
        cols = pl.ds(pl.multiple_of(on_x(i) * feats, feats), feats)
        for j in range(owners):
            start = j * piece
            wg_ref[pl.ds(pl.multiple_of(c * half + start, piece), piece), cols] = ag[i, c, j]
    for d in range(1, ns):
        other = on_sub(d)
        for i in range(nx):
            cols = pl.ds(pl.multiple_of(on_x(i) * feats, feats), feats)
            for j in range(owners):
                remote(
                    ag.at[i, c, j], ag.at[i, other, j], f_send.at[i, d - 1, j], f_recv.at[i, other, j], {"sub": other}
                ).wait_recv()
                start = j * piece
                wg_ref[pl.ds(pl.multiple_of(other * half + start, piece), piece), cols] = ag[i, other, j]
    for side in range(2):
        @pl.when(has[side])
        def _():
            halo_copy(side).wait_send()
            grad_copy(side).wait_send()
    for copy in x_copies:
        copy.wait_send()
    for i in range(nx):
        for d in range(1, ns):
            pair_copy(d, i).wait_send()
        for j in range(owners):
            @pl.when(z != j)
            def _():
                piece_out(i, j).wait_send()

    def owner_sent():
        for i in range(nx):
            for d in range(1, nz):
                to_owner_peer(i, d).wait_send()

    if owners == nz:
        owner_sent()
    else:
        pl.when(z < owners)(owner_sent)
    for i in range(nx):
        for d in range(1, ns):
            for j in range(owners):
                to_core(i, j, d).wait_send()


def deliver(dq_ref, dk_ref, dv_ref, wg_ref, dq_out, dk_out, dv_out, wg_out, wide, sem):
    copies = [
        pltpu.make_async_copy(dq_ref, dq_out, sem.at[0]),
        pltpu.make_async_copy(dk_ref, dk_out, sem.at[1]),
        pltpu.make_async_copy(dv_ref, dv_out, sem.at[2]),
        pltpu.make_async_copy(wide, wg_out, sem.at[3]),
    ]
    for copy in copies[:3]:
        copy.start()
    wide[...] = wg_ref[...].astype(F32)
    copies[3].start()
    for copy in copies:
        copy.wait()


def solution(mesh):
    nz, nx, ns = mesh.shape["nodes"], mesh.shape["heads"], mesh.shape["sub"]

    def on_device(
        queries, key_vectors, value_vectors, cotangent, out_weight, neighbours, entry_mask, live_counts, tile_slot
    ):
        rows, feats = queries.shape
        width = out_weight.shape[1]
        tiles, heads = rows // TILE, feats // HD
        keys = (tiles + 2) * TILE
        half = feats // ns
        owners = min(nz, half // 16)
        piece = half // owners
        vmem, hbm = pl.BlockSpec(memory_space=pltpu.VMEM), pl.BlockSpec(memory_space=pltpu.HBM)
        dma = pltpu.SemaphoreType.DMA
        partial = pl.pallas_call(
            functools.partial(kernel, (nz, nx, ns, owners)),
            out_shape=(
                jax.ShapeDtypeStruct((rows, feats), BF16),
                jax.ShapeDtypeStruct((rows, feats), BF16),
                jax.ShapeDtypeStruct((rows, feats), BF16),
                jax.ShapeDtypeStruct((feats, width), BF16),
            ),
            in_specs=[hbm] * 9,
            out_specs=(vmem,) * 4,
            scratch_shapes=[
                pltpu.SMEM(neighbours.shape, jnp.int32),
                pltpu.SMEM(entry_mask.shape, jnp.int32),
                pltpu.SMEM(live_counts.shape, jnp.int32),
                pltpu.SMEM(tile_slot.shape, jnp.int32),
                pltpu.VMEM((rows, feats), BF16),
                pltpu.VMEM((rows, feats), BF16),
                pltpu.VMEM((rows, feats), BF16),
                pltpu.VMEM((feats, width), BF16),
                dma((9,)),
                pltpu.VMEM((nx, rows, feats), BF16),
                pltpu.VMEM((2, 2, TILE, feats), BF16),
                pltpu.VMEM((2, 2, TILE, feats), BF16),
                pltpu.VMEM((2, 2, TILE, feats), BF16),
                pltpu.VMEM((2, 2, TILE, feats), BF16),
                pltpu.VMEM((heads, LANES, rows), BF16),
                pltpu.VMEM((heads, rows, LANES), BF16),
                pltpu.VMEM((heads, LANES, rows), BF16),
                pltpu.VMEM((heads, rows, LANES), BF16),
                pltpu.VMEM((feats, keys), BF16),
                pltpu.VMEM((feats, keys), BF16),
                pltpu.VMEM((feats, rows), BF16),
                pltpu.VMEM((heads, keys, rows), F32),
                pltpu.VMEM((keys, heads * rows), BF16),
                pltpu.VMEM((keys, heads * rows), BF16),
                pltpu.VMEM((ns - 1, nx, half, feats), BF16),
                pltpu.VMEM((ns - 1, nx, half, feats), BF16),
                pltpu.VMEM((nx, owners, piece, feats), BF16),
                pltpu.VMEM((nx, nz, piece, feats), BF16),
                pltpu.VMEM((nx, ns, owners, piece, feats), BF16),
                pltpu.VMEM((2, heads, 1, rows), F32),
                dma((nx,)), dma((nx,)),
                dma((2,)), dma((2,)),
                dma((2,)), dma((2,)),
                dma((ns - 1, nx)), dma((ns - 1, nx)),
                dma((nx, owners)), dma((nx, nz)),
                dma((nx, nz)), dma((nx, owners)),
                dma((nx, ns - 1, owners)), dma((nx, ns, owners)),
            ],
            compiler_params=pltpu.CompilerParams(
                collective_id=0, has_side_effects=True, vmem_limit_bytes=48 * 1024 * 1024
            ),
        )(
            *(
                pltpu.with_memory_space_constraint(array, pltpu.HBM)
                for array in (
                    neighbours, entry_mask, live_counts, tile_slot,
                    queries, key_vectors, value_vectors, cotangent, out_weight,
                )
            )
        )
        return pl.pallas_call(
            deliver,
            out_shape=(
                jax.ShapeDtypeStruct((rows, feats), BF16),
                jax.ShapeDtypeStruct((rows, feats), BF16),
                jax.ShapeDtypeStruct((rows, feats), BF16),
                jax.ShapeDtypeStruct((feats, width), F32),
            ),
            in_specs=[vmem] * 4,
            out_specs=(hbm,) * 4,
            scratch_shapes=[pltpu.VMEM((feats, width), F32), dma((4,))],
            compiler_params=pltpu.CompilerParams(vmem_limit_bytes=4 * 1024 * 1024),
        )(*partial)

    part = P(("groups", "nodes", "sub"), "heads")
    return jax.shard_map(
        on_device,
        mesh=mesh,
        in_specs=(
            part, part, part, part, P("heads", None), P("groups", None), P("groups", None), P("groups"), P("groups"),
        ),
        out_specs=(part, part, part, P(("groups", "heads"), None)),
        check_vma=False,
    )
```

```python
import functools

import jax
import jax.numpy as jnp
from jax import lax
from jax.experimental import pallas as pl
from jax.experimental.pallas import tpu as pltpu
from jax.sharding import PartitionSpec as P

HD = 64
TILE = 128
LANES = 128
HIDDEN = -1e30
MESH = pl.DeviceIdType.MESH
F32 = jnp.float32
BF16 = jnp.bfloat16


def mm(a, b):
    return jnp.dot(a, b, preferred_element_type=F32)


def mm_nt(a, b):
    return lax.dot_general(a, b, (((1,), (1,)), ((), ())), preferred_element_type=F32)


def turned(value):
    return jnp.transpose(value.astype(F32))


def kernel(
    sizes,
    nb_hbm, mask_hbm, live_hbm, slot_hbm,
    q_hbm, k_hbm, v_hbm, cot_ref, w_hbm,
    dq_ref, dk_ref, dv_ref, wg_ref,
    nb_ref, mask_ref, live_ref, slot_ref, q_ref, k_ref, v_ref, w_ref, in_sem,
    cotg, hsend, halo, gsend, grecv, qt, qm, dot_t, dom, kt, vt, att, pf, pb, sb, wsend, wrecv, zsend, zrecv, ag, stat,
    x_send, x_recv, h_send, h_recv, g_send, g_recv, p_send, p_recv, z_send, z_recv, a_send, a_recv, f_send, f_recv,
):
    nz, nx, ns, owners = sizes
    rows, feats = q_ref.shape
    tiles = rows // TILE
    heads = feats // HD
    pairs = feats // LANES
    per = LANES // HD
    shards = nz * ns
    half = feats // ns
    piece = half // owners
    degree = nb_ref.shape[1]
    total_nodes = rows * shards
    z, x, c = lax.axis_index("nodes"), lax.axis_index("heads"), lax.axis_index("sub")
    s = z * ns + c
    up, down = jnp.minimum(s + 1, shards - 1), jnp.maximum(s - 1, 0)
    has = (s > 0, s < shards - 1)
    sides = (down, up)

    def at_shard(index):
        return {"nodes": lax.div(index, ns), "sub": lax.rem(index, ns)}

    def on_x(d):
        return lax.rem(x + d, nx)

    def on_z(d):
        return lax.rem(z + d, nz)

    def on_sub(d):
        return lax.rem(c + d, ns)

    cross = (jnp.logical_and(c == 0, z > 0), jnp.logical_and(c == ns - 1, z < nz - 1))

    def load(index):
        return pltpu.make_async_copy(*incoming[index], in_sem.at[index])

    incoming = (
        (nb_hbm, nb_ref), (slot_hbm, slot_ref), (k_hbm, k_ref), (v_hbm, v_ref), (mask_hbm, mask_ref),
        (live_hbm, live_ref), (q_hbm, q_ref), (cot_ref, cotg.at[x]), (w_hbm, w_ref),
    )
    for i in range(len(incoming)):
        load(i).start()
    barrier = pltpu.get_barrier_semaphore()

    def greet(device):
        pl.semaphore_signal(barrier, inc=1, device_id=device, device_id_type=MESH)

    for d in range(1, nx):
        greet({"heads": on_x(d)})
    for d in range(1, ns):
        greet({"sub": on_sub(d)})
    for side in range(2):
        @pl.when(cross[side])
        def _():
            greet(at_shard(sides[side]))
    for d in range(1, nz):
        greet({"nodes": on_z(d)})

    load(0).wait()
    load(1).wait()
    chosen = []
    for side in range(2):
        pick = jnp.int32(0)
        for r in range(tiles):
            for e in range(degree):
                slot = slot_ref[nb_ref[sides[side] * tiles + r, e]]
                local = slot - s * tiles
                inside = jnp.logical_and(local >= 0, local < tiles)
                pick = jnp.where(inside, local, pick)
        chosen.append(pick)
    load(2).wait()
    load(3).wait()
    for side in range(2):
        kk, vv = k_ref[0:TILE, :], v_ref[0:TILE, :]
        for t in range(1, tiles):
            here = chosen[side] == t
            kk = jnp.where(here, k_ref[t * TILE : (t + 1) * TILE, :], kk)
            vv = jnp.where(here, v_ref[t * TILE : (t + 1) * TILE, :], vv)
        hsend[side, 0] = kk
        hsend[side, 1] = vv

    extra = jnp.where(jnp.logical_or(cross[0], cross[1]), 1, 0)
    pl.semaphore_wait(barrier, nx - 1 + ns - 1 + nz - 1 + extra)

    def remote(src, dst, send, recv, device):
        return pltpu.make_async_remote_copy(
            src_ref=src, dst_ref=dst, send_sem=send, recv_sem=recv, device_id=device, device_id_type=MESH
        )

    def halo_copy(side, which):
        return remote(
            hsend.at[side, which], halo.at[1 - side, which], h_send.at[side, which], h_recv.at[1 - side, which],
            at_shard(sides[side]),
        )

    def halo_wait(side, which):
        return remote(
            hsend.at[side, which], halo.at[side, which], h_send.at[side, which], h_recv.at[side, which],
            at_shard(sides[side]),
        )

    def grad_copy(side):
        return remote(gsend.at[side], grecv.at[1 - side], g_send.at[side], g_recv.at[1 - side], at_shard(sides[side]))

    def grad_wait(side):
        return remote(gsend.at[side], grecv.at[side], g_send.at[side], g_recv.at[side], at_shard(sides[side]))

    for which in range(2):
        for side in range(2):
            @pl.when(has[side])
            def _():
                halo_copy(side, which).start()

    x_copies = [
        remote(cot_ref, cotg.at[x], x_send.at[d], x_recv.at[x], {"heads": on_x(d)}) for d in range(1, nx)
    ]
    for copy in x_copies:
        copy.start()
    for side in range(2):
        @pl.when(jnp.logical_not(has[side]))
        def _():
            halo[side] = jnp.zeros(halo.shape[1:], BF16)
            grecv[side] = jnp.zeros(grecv.shape[1:], BF16)

    load(4).wait()
    load(5).wait()
    live = live_ref[s]
    counts = []
    for r in range(tiles):
        seen = [jnp.int32(0)] * (tiles + 2)
        for e in range(degree):
            local = slot_ref[nb_ref[s * tiles + r, e]] - s * tiles
            good = jnp.where(mask_ref[s * tiles + r, e] == 1, 1, 0)
            for t in range(tiles):
                seen[t] = seen[t] + jnp.where(local == t, good, 0)
            seen[tiles] = seen[tiles] + jnp.where(local < 0, good, 0)
            seen[tiles + 1] = seen[tiles + 1] + jnp.where(local >= tiles, good, 0)
        counts.append([jnp.where(r < live, n, 0) for n in seen])
    biases = [[jnp.where(n > 0, 0.0, HIDDEN).astype(F32) for n in row] for row in counts]
    counts = [[n.astype(F32) for n in row] for row in counts]

    scale = HD ** (-0.5)
    load(6).wait()
    scaled = q_ref[...].astype(F32) * scale
    lane = lax.broadcasted_iota(jnp.int32, (rows, LANES), 1)
    sub_row = lax.broadcasted_iota(jnp.int32, (LANES, rows), 0)
    q_t = jnp.transpose(scaled)
    for h in range(heads):
        p, i = divmod(h, per)
        mine = jnp.logical_and(sub_row >= i * HD, sub_row < (i + 1) * HD)
        qt[h] = jnp.where(mine, q_t[p * LANES : (p + 1) * LANES, :], 0.0).astype(BF16)
        mine = jnp.logical_and(lane >= i * HD, lane < (i + 1) * HD)
        qm[h] = jnp.where(mine, scaled[:, p * LANES : (p + 1) * LANES], 0.0).astype(BF16)
    own = tiles * TILE
    keys = own + 2 * TILE
    kt[:, 0:own] = turned(k_ref[...]).astype(BF16)
    vt[:, 0:own] = turned(v_ref[...]).astype(BF16)
    for h in range(heads):
        cols = slice((h // per) * LANES, (h // per + 1) * LANES)
        blocks = [mm(k_ref[t * TILE : (t + 1) * TILE, cols], qt[h]) for t in range(tiles)]
        for r in range(tiles):
            span = slice(r * TILE, (r + 1) * TILE)
            parts = [blocks[t][:, span] + biases[r][t] for t in range(tiles)]
            top = functools.reduce(jnp.maximum, [jnp.max(part, axis=0, keepdims=True) for part in parts])
            parts = [jnp.exp(part - top) for part in parts]
            stat[0, h, :, span] = top
            stat[1, h, :, span] = sum(
                jnp.sum(part, axis=0, keepdims=True) * counts[r][t] for t, part in enumerate(parts)
            )
            for t, part in enumerate(parts):
                pf[h, t * TILE : (t + 1) * TILE, span] = part
    for side in range(2):
        @pl.when(has[side])
        def _():
            halo_wait(side, 0).wait_recv()
    def attend(h):
        cols = pl.ds(pl.multiple_of(lax.div(h, per) * LANES, LANES), LANES)
        blocks = [mm(halo[side, 0, :, cols], qt[h]) for side in range(2)]
        for r in range(tiles):
            span = slice(r * TILE, (r + 1) * TILE)
            into = pl.ds(pl.multiple_of(h * rows + r * TILE, TILE), TILE)
            parts = [blocks[side][:, span] + biases[r][tiles + side] for side in range(2)]
            before = stat[0, h, :, span]
            top = functools.reduce(jnp.maximum, [jnp.max(part, axis=0, keepdims=True) for part in parts], before)
            parts = [jnp.exp(part - top) for part in parts]
            shrink = jnp.exp(before - top)
            below = stat[1, h, :, span] * shrink + sum(
                jnp.sum(part, axis=0, keepdims=True) * counts[r][tiles + side] for side, part in enumerate(parts)
            )
            over = 1.0 / jnp.where(below > 0.0, below, 1.0)
            for t in range(tiles + 2):
                lines = slice(t * TILE, (t + 1) * TILE)
                if t < tiles:
                    weight = pf[h, lines, span] * (counts[r][t] * shrink * over)
                else:
                    weight = parts[t - tiles] * (counts[r][t] * over)
                pf[h, lines, span] = weight
                pb[lines, into] = weight.astype(BF16)

    def collect(h):
        lines = pl.ds(pl.multiple_of(h * HD, HD), HD)
        att[lines, :] = mm(vt[lines, :], pb[:, pl.ds(pl.multiple_of(h * rows, rows), rows)]).astype(BF16)

    def weight_rows(index, i):
        return mm(att[pl.ds(pl.multiple_of(index * half, half), half), :], cotg[on_x(i)])

    def pair_copy(d, i):
        return remote(
            wsend.at[d - 1, i], wrecv.at[d - 1, i], p_send.at[d - 1, i], p_recv.at[d - 1, i], {"sub": on_sub(d)}
        )

    def pair_start(d, i):
        wsend[d - 1, i] = weight_rows(on_sub(d), i).astype(BF16)
        pair_copy(d, i).start()

    here = heads // ns
    load(7).wait()
    order = [on_sub(d) * here + i for d in list(range(1, ns)) + [0] for i in range(here)]
    for h in order:
        attend(h)
    for side in range(2):
        @pl.when(has[side])
        def _():
            halo_wait(side, 1).wait_recv()
    for side in range(2):
        at = own + side * TILE
        vt[:, at : at + TILE] = turned(halo[side, 1]).astype(BF16)
    for d in range(1, ns):
        for h in order[(d - 1) * here : d * here]:
            collect(h)
        pair_start(d, 0)
    for h in order[(ns - 1) * here :]:
        collect(h)
    mine_rows = [weight_rows(c, 0)]
    load(8).wait()
    for d in range(1, nx):
        remote(cot_ref, cotg.at[on_x(d)], x_send.at[d], x_recv.at[on_x(d)], {"heads": on_x(d)}).wait_recv()
    for i in range(1, nx):
        for d in range(1, ns):
            pair_start(d, i)
        mine_rows.append(weight_rows(c, i))

    def piece_out(i, j):
        return remote(zsend.at[i, j], zrecv.at[i, z], z_send.at[i, j], z_recv.at[i, z], {"nodes": jnp.int32(j)})

    def spread(i):
        for d in range(1, ns):
            pair_copy(d, i).wait_recv()
        chip = mine_rows[i]
        for d in range(1, ns):
            chip = chip + wrecv[d - 1, i].astype(F32)
        for j in range(owners):
            zsend[i, j] = chip[j * piece : (j + 1) * piece, :].astype(BF16)
        for j in range(owners):
            @pl.when(z != j)
            def _():
                piece_out(i, j).start()

    spread(0)
    dt = sum(mm_nt(w_ref[:, i * feats : (i + 1) * feats], cotg[i]) for i in range(nx)).astype(BF16)
    d_o = turned(dt)
    for h in range(heads):
        p, i = divmod(h, per)
        mine = jnp.logical_and(sub_row >= i * HD, sub_row < (i + 1) * HD)
        dot_t[h] = jnp.where(mine, dt[p * LANES : (p + 1) * LANES, :].astype(F32), 0.0).astype(BF16)
        mine = jnp.logical_and(lane >= i * HD, lane < (i + 1) * HD)
        dom[h] = jnp.where(mine, d_o[:, p * LANES : (p + 1) * LANES], 0.0).astype(BF16)
    product = dt.astype(F32) * att[...].astype(F32)
    deltas = [jnp.sum(product[h * HD : (h + 1) * HD, :], axis=0, keepdims=True) for h in range(heads)]
    for i in range(1, nx):
        spread(i)
    def score_grads(h, t, values):
        part = mm(values, dot_t[h])
        grad = pf[h, t * TILE : (t + 1) * TILE, :] * (part - deltas[h])
        sb[t * TILE : (t + 1) * TILE, h * rows : (h + 1) * rows] = grad.astype(BF16)

    def key_terms(t, p):
        area = slice(p * per * rows, (p + 1) * per * rows)
        lines = slice(t * TILE, (t + 1) * TILE)
        width = per * rows
        k_part = mm(sb[lines, area], qm[p * per : (p + 1) * per].reshape(width, LANES))
        v_part = mm(pb[lines, area], dom[p * per : (p + 1) * per].reshape(width, LANES))
        return k_part, v_part

    for side in range(2):
        for h in range(heads):
            cols = slice((h // per) * LANES, (h // per + 1) * LANES)
            score_grads(h, tiles + side, halo[side, 1, :, cols])
        for p in range(pairs):
            k_part, v_part = key_terms(tiles + side, p)
            gsend[side, 0, :, p * LANES : (p + 1) * LANES] = k_part.astype(BF16)
            gsend[side, 1, :, p * LANES : (p + 1) * LANES] = v_part.astype(BF16)

        @pl.when(has[side])
        def _():
            grad_copy(side).start()

    factor = total_nodes ** (-0.5)

    def piece_in(i, j):
        return remote(zsend.at[i, 0], zrecv.at[i, j], z_send.at[i, 0], z_recv.at[i, j], {"nodes": z})

    def to_owner_peer(i, d):
        return remote(ag.at[i, c, z], ag.at[i, c, z], a_send.at[i, d], a_recv.at[i, z], {"nodes": on_z(d)})

    def to_core(i, j, d):
        return remote(ag.at[i, c, j], ag.at[i, c, j], f_send.at[i, d - 1, j], f_recv.at[i, c, j], {"sub": on_sub(d)})

    def owner_part():
        for i in range(nx):
            acc = zsend[i, z].astype(F32)
            for d in range(1, nz):
                j = on_z(d)
                piece_in(i, j).wait_recv()
                acc = acc + zrecv[i, j].astype(F32)
            ag[i, c, z] = (acc * factor).astype(BF16)
            for d in range(1, nz):
                to_owner_peer(i, d).start()
            for d in range(1, ns):
                to_core(i, z, d).start()

    def forward_part(i, j):
        remote(ag.at[i, c, j], ag.at[i, c, j], a_send.at[i, 0], a_recv.at[i, j], {"nodes": z}).wait_recv()
        for d in range(1, ns):
            to_core(i, j, d).start()

    for side in range(2):
        at = own + side * TILE
        kt[:, at : at + TILE] = turned(halo[side, 0]).astype(BF16)
    if owners == nz:
        owner_part()
    else:
        pl.when(z < owners)(owner_part)

    for t in range(tiles):
        for h in range(heads):
            cols = slice((h // per) * LANES, (h // per + 1) * LANES)
            score_grads(h, t, v_ref[t * TILE : (t + 1) * TILE, cols])
    own_terms = [[key_terms(t, p) for p in range(pairs)] for t in range(tiles)]
    dq_t = jnp.concatenate(
        [mm(kt[h * HD : (h + 1) * HD, :], sb[:, h * rows : (h + 1) * rows]) for h in range(heads)], axis=0
    )
    dq_ref[...] = (jnp.transpose(dq_t) * scale).astype(BF16)


    for side in range(2):
        @pl.when(has[side])
        def _():
            grad_wait(side).wait_recv()
    for t in range(tiles):
        lines = slice(t * TILE, (t + 1) * TILE)
        gates = [jnp.where(chosen[side] == t, 1.0, 0.0).astype(F32) for side in range(2)]
        for p in range(pairs):
            cols = slice(p * LANES, (p + 1) * LANES)
            for which, out in ((0, dk_ref), (1, dv_ref)):
                value = own_terms[t][p][which]
                for side in range(2):
                    value = value + grecv[side, which, :, cols].astype(F32) * gates[side]
                out[lines, cols] = value.astype(BF16)

    for i in range(nx):
        for j in range(owners):
            @pl.when(z != j)
            def _():
                forward_part(i, j)
    for i in range(nx):
        cols = pl.ds(pl.multiple_of(on_x(i) * feats, feats), feats)
        for j in range(owners):
            start = j * piece
            wg_ref[pl.ds(pl.multiple_of(c * half + start, piece), piece), cols] = ag[i, c, j]
    for d in range(1, ns):
        other = on_sub(d)
        for i in range(nx):
            cols = pl.ds(pl.multiple_of(on_x(i) * feats, feats), feats)
            for j in range(owners):
                remote(
                    ag.at[i, c, j], ag.at[i, other, j], f_send.at[i, d - 1, j], f_recv.at[i, other, j], {"sub": other}
                ).wait_recv()
                start = j * piece
                wg_ref[pl.ds(pl.multiple_of(other * half + start, piece), piece), cols] = ag[i, other, j]
    for side in range(2):
        @pl.when(has[side])
        def _():
            for which in range(2):
                halo_copy(side, which).wait_send()
            grad_copy(side).wait_send()
    for copy in x_copies:
        copy.wait_send()
    for i in range(nx):
        for d in range(1, ns):
            pair_copy(d, i).wait_send()
        for j in range(owners):
            @pl.when(z != j)
            def _():
                piece_out(i, j).wait_send()

    def owner_sent():
        for i in range(nx):
            for d in range(1, nz):
                to_owner_peer(i, d).wait_send()

    if owners == nz:
        owner_sent()
    else:
        pl.when(z < owners)(owner_sent)
    for i in range(nx):
        for d in range(1, ns):
            for j in range(owners):
                to_core(i, j, d).wait_send()


def deliver(dq_ref, dk_ref, dv_ref, wg_ref, dq_out, dk_out, dv_out, wg_out, wide, sem):
    copies = [
        pltpu.make_async_copy(dq_ref, dq_out, sem.at[0]),
        pltpu.make_async_copy(dk_ref, dk_out, sem.at[1]),
        pltpu.make_async_copy(dv_ref, dv_out, sem.at[2]),
        pltpu.make_async_copy(wide, wg_out, sem.at[3]),
    ]
    for copy in copies[:3]:
        copy.start()
    wide[...] = wg_ref[...].astype(F32)
    copies[3].start()
    for copy in copies:
        copy.wait()


def solution(mesh):
    nz, nx, ns = mesh.shape["nodes"], mesh.shape["heads"], mesh.shape["sub"]

    def on_device(
        queries, key_vectors, value_vectors, cotangent, out_weight, neighbours, entry_mask, live_counts, tile_slot
    ):
        rows, feats = queries.shape
        width = out_weight.shape[1]
        tiles, heads = rows // TILE, feats // HD
        keys = (tiles + 2) * TILE
        half = feats // ns
        owners = min(nz, half // 16)
        piece = half // owners
        vmem, hbm = pl.BlockSpec(memory_space=pltpu.VMEM), pl.BlockSpec(memory_space=pltpu.HBM)
        dma = pltpu.SemaphoreType.DMA
        partial = pl.pallas_call(
            functools.partial(kernel, (nz, nx, ns, owners)),
            out_shape=(
                jax.ShapeDtypeStruct((rows, feats), BF16),
                jax.ShapeDtypeStruct((rows, feats), BF16),
                jax.ShapeDtypeStruct((rows, feats), BF16),
                jax.ShapeDtypeStruct((feats, width), BF16),
            ),
            in_specs=[hbm] * 9,
            out_specs=(vmem,) * 4,
            scratch_shapes=[
                pltpu.SMEM(neighbours.shape, jnp.int32),
                pltpu.SMEM(entry_mask.shape, jnp.int32),
                pltpu.SMEM(live_counts.shape, jnp.int32),
                pltpu.SMEM(tile_slot.shape, jnp.int32),
                pltpu.VMEM((rows, feats), BF16),
                pltpu.VMEM((rows, feats), BF16),
                pltpu.VMEM((rows, feats), BF16),
                pltpu.VMEM((feats, width), BF16),
                dma((9,)),
                pltpu.VMEM((nx, rows, feats), BF16),
                pltpu.VMEM((2, 2, TILE, feats), BF16),
                pltpu.VMEM((2, 2, TILE, feats), BF16),
                pltpu.VMEM((2, 2, TILE, feats), BF16),
                pltpu.VMEM((2, 2, TILE, feats), BF16),
                pltpu.VMEM((heads, LANES, rows), BF16),
                pltpu.VMEM((heads, rows, LANES), BF16),
                pltpu.VMEM((heads, LANES, rows), BF16),
                pltpu.VMEM((heads, rows, LANES), BF16),
                pltpu.VMEM((feats, keys), BF16),
                pltpu.VMEM((feats, keys), BF16),
                pltpu.VMEM((feats, rows), BF16),
                pltpu.VMEM((heads, keys, rows), F32),
                pltpu.VMEM((keys, heads * rows), BF16),
                pltpu.VMEM((keys, heads * rows), BF16),
                pltpu.VMEM((ns - 1, nx, half, feats), BF16),
                pltpu.VMEM((ns - 1, nx, half, feats), BF16),
                pltpu.VMEM((nx, owners, piece, feats), BF16),
                pltpu.VMEM((nx, nz, piece, feats), BF16),
                pltpu.VMEM((nx, ns, owners, piece, feats), BF16),
                pltpu.VMEM((2, heads, 1, rows), F32),
                dma((nx,)), dma((nx,)),
                dma((2, 2)), dma((2, 2)),
                dma((2,)), dma((2,)),
                dma((ns - 1, nx)), dma((ns - 1, nx)),
                dma((nx, owners)), dma((nx, nz)),
                dma((nx, nz)), dma((nx, owners)),
                dma((nx, ns - 1, owners)), dma((nx, ns, owners)),
            ],
            compiler_params=pltpu.CompilerParams(
                collective_id=0, has_side_effects=True, vmem_limit_bytes=48 * 1024 * 1024
            ),
        )(
            *(
                pltpu.with_memory_space_constraint(array, pltpu.HBM)
                for array in (
                    neighbours, entry_mask, live_counts, tile_slot,
                    queries, key_vectors, value_vectors, cotangent, out_weight,
                )
            )
        )
        return pl.pallas_call(
            deliver,
            out_shape=(
                jax.ShapeDtypeStruct((rows, feats), BF16),
                jax.ShapeDtypeStruct((rows, feats), BF16),
                jax.ShapeDtypeStruct((rows, feats), BF16),
                jax.ShapeDtypeStruct((feats, width), F32),
            ),
            in_specs=[vmem] * 4,
            out_specs=(hbm,) * 4,
            scratch_shapes=[pltpu.VMEM((feats, width), F32), dma((4,))],
            compiler_params=pltpu.CompilerParams(vmem_limit_bytes=4 * 1024 * 1024),
        )(*partial)

    part = P(("groups", "nodes", "sub"), "heads")
    return jax.shard_map(
        on_device,
        mesh=mesh,
        in_specs=(
            part, part, part, part, P("heads", None), P("groups", None), P("groups", None), P("groups"), P("groups"),
        ),
        out_specs=(part, part, part, P(("groups", "heads"), None)),
        check_vma=False,
    )
```

```python
import functools

import jax
import jax.numpy as jnp
from jax import lax
from jax.experimental import pallas as pl
from jax.experimental.pallas import tpu as pltpu
from jax.sharding import PartitionSpec as P

HD = 64
TILE = 128
LANES = 128
HIDDEN = -1e30
MESH = pl.DeviceIdType.MESH
F32 = jnp.float32
BF16 = jnp.bfloat16


def mm(a, b):
    return jnp.dot(a, b, preferred_element_type=F32)


def mm_nt(a, b):
    return lax.dot_general(a, b, (((1,), (1,)), ((), ())), preferred_element_type=F32)


def turned(value):
    return jnp.transpose(value.astype(F32))


def kernel(
    sizes,
    nb_hbm, mask_hbm, live_hbm, slot_hbm,
    q_hbm, k_hbm, v_hbm, cot_ref, w_hbm,
    dq_ref, dk_ref, dv_ref, wg_ref,
    nb_ref, mask_ref, live_ref, slot_ref, q_ref, k_ref, v_ref, w_ref, in_sem,
    cotg, hsend, halo, gsend, grecv, qt, qm, dot_t, dom, kt, vt, att, pf, pb, sb, wsend, wrecv, zsend, zrecv, ag, stat,
    x_send, x_recv, h_send, h_recv, g_send, g_recv, p_send, p_recv, z_send, z_recv, a_send, a_recv, f_send, f_recv,
):
    nz, nx, ns, owners = sizes
    rows, feats = q_ref.shape
    tiles = rows // TILE
    heads = feats // HD
    pairs = feats // LANES
    per = LANES // HD
    shards = nz * ns
    half = feats // ns
    piece = half // owners
    degree = nb_ref.shape[1]
    total_nodes = rows * shards
    z, x, c = lax.axis_index("nodes"), lax.axis_index("heads"), lax.axis_index("sub")
    s = z * ns + c
    up, down = jnp.minimum(s + 1, shards - 1), jnp.maximum(s - 1, 0)
    has = (s > 0, s < shards - 1)
    sides = (down, up)

    def at_shard(index):
        return {"nodes": lax.div(index, ns), "sub": lax.rem(index, ns)}

    def on_x(d):
        return lax.rem(x + d, nx)

    def on_z(d):
        return lax.rem(z + d, nz)

    def on_sub(d):
        return lax.rem(c + d, ns)

    cross = (jnp.logical_and(c == 0, z > 0), jnp.logical_and(c == ns - 1, z < nz - 1))

    def load(index):
        return pltpu.make_async_copy(*incoming[index], in_sem.at[index])

    incoming = (
        (nb_hbm, nb_ref), (slot_hbm, slot_ref), (k_hbm, k_ref), (v_hbm, v_ref), (mask_hbm, mask_ref),
        (live_hbm, live_ref), (q_hbm, q_ref), (cot_ref, cotg.at[x]), (w_hbm, w_ref),
    )
    for i in range(len(incoming)):
        load(i).start()
    barrier = pltpu.get_barrier_semaphore()

    def greet(device):
        pl.semaphore_signal(barrier, inc=1, device_id=device, device_id_type=MESH)

    for d in range(1, nx):
        greet({"heads": on_x(d)})
    for d in range(1, ns):
        greet({"sub": on_sub(d)})
    for side in range(2):
        @pl.when(cross[side])
        def _():
            greet(at_shard(sides[side]))
    for d in range(1, nz):
        greet({"nodes": on_z(d)})

    load(0).wait()
    load(1).wait()
    chosen = []
    for side in range(2):
        pick = jnp.int32(0)
        for r in range(tiles):
            for e in range(degree):
                slot = slot_ref[nb_ref[sides[side] * tiles + r, e]]
                local = slot - s * tiles
                inside = jnp.logical_and(local >= 0, local < tiles)
                pick = jnp.where(inside, local, pick)
        chosen.append(pick)
    load(2).wait()
    load(3).wait()
    for side in range(2):
        kk, vv = k_ref[0:TILE, :], v_ref[0:TILE, :]
        for t in range(1, tiles):
            here = chosen[side] == t
            kk = jnp.where(here, k_ref[t * TILE : (t + 1) * TILE, :], kk)
            vv = jnp.where(here, v_ref[t * TILE : (t + 1) * TILE, :], vv)
        hsend[side, 0] = kk
        hsend[side, 1] = vv

    extra = jnp.where(jnp.logical_or(cross[0], cross[1]), 1, 0)
    pl.semaphore_wait(barrier, nx - 1 + ns - 1 + nz - 1 + extra)

    def remote(src, dst, send, recv, device):
        return pltpu.make_async_remote_copy(
            src_ref=src, dst_ref=dst, send_sem=send, recv_sem=recv, device_id=device, device_id_type=MESH
        )

    def halo_copy(side, which):
        return remote(
            hsend.at[side, which], halo.at[1 - side, which], h_send.at[side, which], h_recv.at[1 - side, which],
            at_shard(sides[side]),
        )

    def halo_wait(side, which):
        return remote(
            hsend.at[side, which], halo.at[side, which], h_send.at[side, which], h_recv.at[side, which],
            at_shard(sides[side]),
        )

    def grad_copy(side):
        return remote(gsend.at[side], grecv.at[1 - side], g_send.at[side], g_recv.at[1 - side], at_shard(sides[side]))

    def grad_wait(side):
        return remote(gsend.at[side], grecv.at[side], g_send.at[side], g_recv.at[side], at_shard(sides[side]))

    for which in range(2):
        for side in range(2):
            @pl.when(has[side])
            def _():
                halo_copy(side, which).start()

    x_copies = [
        remote(cot_ref, cotg.at[x], x_send.at[d], x_recv.at[x], {"heads": on_x(d)}) for d in range(1, nx)
    ]
    for copy in x_copies:
        copy.start()
    for side in range(2):
        @pl.when(jnp.logical_not(has[side]))
        def _():
            halo[side] = jnp.zeros(halo.shape[1:], BF16)
            grecv[side] = jnp.zeros(grecv.shape[1:], BF16)

    load(4).wait()
    load(5).wait()
    live = live_ref[s]
    counts = []
    for r in range(tiles):
        seen = [jnp.int32(0)] * (tiles + 2)
        for e in range(degree):
            local = slot_ref[nb_ref[s * tiles + r, e]] - s * tiles
            good = jnp.where(mask_ref[s * tiles + r, e] == 1, 1, 0)
            for t in range(tiles):
                seen[t] = seen[t] + jnp.where(local == t, good, 0)
            seen[tiles] = seen[tiles] + jnp.where(local < 0, good, 0)
            seen[tiles + 1] = seen[tiles + 1] + jnp.where(local >= tiles, good, 0)
        counts.append([jnp.where(r < live, n, 0) for n in seen])
    biases = [[jnp.where(n > 0, 0.0, HIDDEN).astype(F32) for n in row] for row in counts]
    counts = [[n.astype(F32) for n in row] for row in counts]

    scale = HD ** (-0.5)
    load(6).wait()
    scaled = q_ref[...].astype(F32) * scale
    lane = lax.broadcasted_iota(jnp.int32, (rows, LANES), 1)
    sub_row = lax.broadcasted_iota(jnp.int32, (LANES, rows), 0)
    q_t = jnp.transpose(scaled)
    for h in range(heads):
        p, i = divmod(h, per)
        mine = jnp.logical_and(sub_row >= i * HD, sub_row < (i + 1) * HD)
        qt[h] = jnp.where(mine, q_t[p * LANES : (p + 1) * LANES, :], 0.0).astype(BF16)
        mine = jnp.logical_and(lane >= i * HD, lane < (i + 1) * HD)
        qm[h] = jnp.where(mine, scaled[:, p * LANES : (p + 1) * LANES], 0.0).astype(BF16)
    own = tiles * TILE
    keys = own + 2 * TILE
    kt[:, 0:own] = turned(k_ref[...]).astype(BF16)
    vt[:, 0:own] = turned(v_ref[...]).astype(BF16)
    for h in range(heads):
        cols = slice((h // per) * LANES, (h // per + 1) * LANES)
        blocks = [mm(k_ref[t * TILE : (t + 1) * TILE, cols], qt[h]) for t in range(tiles)]
        for r in range(tiles):
            span = slice(r * TILE, (r + 1) * TILE)
            parts = [blocks[t][:, span] + biases[r][t] for t in range(tiles)]
            top = functools.reduce(jnp.maximum, [jnp.max(part, axis=0, keepdims=True) for part in parts])
            parts = [jnp.exp(part - top) for part in parts]
            stat[0, h, :, span] = top
            stat[1, h, :, span] = sum(
                jnp.sum(part, axis=0, keepdims=True) * counts[r][t] for t, part in enumerate(parts)
            )
            for t, part in enumerate(parts):
                pf[h, t * TILE : (t + 1) * TILE, span] = part
    for side in range(2):
        @pl.when(has[side])
        def _():
            halo_wait(side, 0).wait_recv()
    def attend(h):
        cols = pl.ds(pl.multiple_of(lax.div(h, per) * LANES, LANES), LANES)
        blocks = [mm(halo[side, 0, :, cols], qt[h]) for side in range(2)]
        for r in range(tiles):
            span = slice(r * TILE, (r + 1) * TILE)
            into = pl.ds(pl.multiple_of(h * rows + r * TILE, TILE), TILE)
            parts = [blocks[side][:, span] + biases[r][tiles + side] for side in range(2)]
            before = stat[0, h, :, span]
            top = functools.reduce(jnp.maximum, [jnp.max(part, axis=0, keepdims=True) for part in parts], before)
            parts = [jnp.exp(part - top) for part in parts]
            shrink = jnp.exp(before - top)
            below = stat[1, h, :, span] * shrink + sum(
                jnp.sum(part, axis=0, keepdims=True) * counts[r][tiles + side] for side, part in enumerate(parts)
            )
            over = 1.0 / jnp.where(below > 0.0, below, 1.0)
            for t in range(tiles + 2):
                lines = slice(t * TILE, (t + 1) * TILE)
                if t < tiles:
                    weight = pf[h, lines, span] * (counts[r][t] * shrink * over)
                else:
                    weight = parts[t - tiles] * (counts[r][t] * over)
                pf[h, lines, span] = weight
                pb[lines, into] = weight.astype(BF16)

    def collect(h):
        lines = pl.ds(pl.multiple_of(h * HD, HD), HD)
        att[lines, :] = mm(vt[lines, :], pb[:, pl.ds(pl.multiple_of(h * rows, rows), rows)]).astype(BF16)

    def weight_rows(index, i):
        return mm(att[pl.ds(pl.multiple_of(index * half, half), half), :], cotg[on_x(i)])

    def pair_copy(d, i):
        return remote(
            wsend.at[d - 1, i], wrecv.at[d - 1, i], p_send.at[d - 1, i], p_recv.at[d - 1, i], {"sub": on_sub(d)}
        )

    def pair_start(d, i):
        wsend[d - 1, i] = weight_rows(on_sub(d), i).astype(BF16)
        pair_copy(d, i).start()

    here = heads // ns
    load(7).wait()
    order = [on_sub(d) * here + i for d in list(range(1, ns)) + [0] for i in range(here)]
    for h in order:
        attend(h)
    for side in range(2):
        @pl.when(has[side])
        def _():
            halo_wait(side, 1).wait_recv()
    for side in range(2):
        at = own + side * TILE
        vt[:, at : at + TILE] = turned(halo[side, 1]).astype(BF16)
    for d in range(1, ns):
        for h in order[(d - 1) * here : d * here]:
            collect(h)
        pair_start(d, 0)
    for h in order[(ns - 1) * here :]:
        collect(h)
    mine_rows = [weight_rows(c, 0)]
    load(8).wait()
    for d in range(1, nx):
        remote(cot_ref, cotg.at[on_x(d)], x_send.at[d], x_recv.at[on_x(d)], {"heads": on_x(d)}).wait_recv()
    for i in range(1, nx):
        for d in range(1, ns):
            pair_start(d, i)
        mine_rows.append(weight_rows(c, i))

    def along_z(act, limit, distances):
        for distance in distances:
            for j in (z + distance, z - distance):
                pl.when(jnp.logical_and(j >= 0, j < limit))(functools.partial(act, j))

    near, far = range(1, nz), range(nz - 1, 0, -1)

    def piece_out(i, j):
        return remote(zsend.at[i, j], zrecv.at[i, z], z_send.at[i, j], z_recv.at[i, z], {"nodes": j})

    def spread(i):
        for d in range(1, ns):
            pair_copy(d, i).wait_recv()
        chip = mine_rows[i]
        for d in range(1, ns):
            chip = chip + wrecv[d - 1, i].astype(F32)
        for j in range(owners):
            zsend[i, j] = chip[j * piece : (j + 1) * piece, :].astype(BF16)
        along_z(lambda j: piece_out(i, j).start(), owners, far)

    spread(0)
    dt = sum(mm_nt(w_ref[:, i * feats : (i + 1) * feats], cotg[i]) for i in range(nx)).astype(BF16)
    d_o = turned(dt)
    for h in range(heads):
        p, i = divmod(h, per)
        mine = jnp.logical_and(sub_row >= i * HD, sub_row < (i + 1) * HD)
        dot_t[h] = jnp.where(mine, dt[p * LANES : (p + 1) * LANES, :].astype(F32), 0.0).astype(BF16)
        mine = jnp.logical_and(lane >= i * HD, lane < (i + 1) * HD)
        dom[h] = jnp.where(mine, d_o[:, p * LANES : (p + 1) * LANES], 0.0).astype(BF16)
    product = dt.astype(F32) * att[...].astype(F32)
    deltas = [jnp.sum(product[h * HD : (h + 1) * HD, :], axis=0, keepdims=True) for h in range(heads)]
    for i in range(1, nx):
        spread(i)
    def score_grads(h, t, values):
        part = mm(values, dot_t[h])
        grad = pf[h, t * TILE : (t + 1) * TILE, :] * (part - deltas[h])
        sb[t * TILE : (t + 1) * TILE, h * rows : (h + 1) * rows] = grad.astype(BF16)

    def key_terms(t, p):
        area = slice(p * per * rows, (p + 1) * per * rows)
        lines = slice(t * TILE, (t + 1) * TILE)
        width = per * rows
        k_part = mm(sb[lines, area], qm[p * per : (p + 1) * per].reshape(width, LANES))
        v_part = mm(pb[lines, area], dom[p * per : (p + 1) * per].reshape(width, LANES))
        return k_part, v_part

    for side in range(2):
        for h in range(heads):
            cols = slice((h // per) * LANES, (h // per + 1) * LANES)
            score_grads(h, tiles + side, halo[side, 1, :, cols])
        for p in range(pairs):
            k_part, v_part = key_terms(tiles + side, p)
            gsend[side, 0, :, p * LANES : (p + 1) * LANES] = k_part.astype(BF16)
            gsend[side, 1, :, p * LANES : (p + 1) * LANES] = v_part.astype(BF16)

        @pl.when(has[side])
        def _():
            grad_copy(side).start()

    factor = total_nodes ** (-0.5)

    def piece_in(i, j):
        return remote(zsend.at[i, 0], zrecv.at[i, j], z_send.at[i, 0], z_recv.at[i, j], {"nodes": z})

    def to_owner_peer(i, j):
        return remote(ag.at[i, c, z], ag.at[i, c, z], a_send.at[i, j], a_recv.at[i, z], {"nodes": j})

    def to_core(i, j, d):
        return remote(ag.at[i, c, j], ag.at[i, c, j], f_send.at[i, d - 1, j], f_recv.at[i, c, j], {"sub": on_sub(d)})

    def owner_part():
        for i in range(nx):
            acc = zsend[i, z].astype(F32)
            for d in range(1, nz):
                j = on_z(d)
                piece_in(i, j).wait_recv()
                acc = acc + zrecv[i, j].astype(F32)
            ag[i, c, z] = (acc * factor).astype(BF16)
            along_z(lambda j: to_owner_peer(i, j).start(), nz, far)
            for d in range(1, ns):
                to_core(i, z, d).start()

    def forward_part(i, j):
        remote(ag.at[i, c, j], ag.at[i, c, j], a_send.at[i, 0], a_recv.at[i, j], {"nodes": z}).wait_recv()
        for d in range(1, ns):
            to_core(i, j, d).start()

    for side in range(2):
        at = own + side * TILE
        kt[:, at : at + TILE] = turned(halo[side, 0]).astype(BF16)
    if owners == nz:
        owner_part()
    else:
        pl.when(z < owners)(owner_part)

    for t in range(tiles):
        for h in range(heads):
            cols = slice((h // per) * LANES, (h // per + 1) * LANES)
            score_grads(h, t, v_ref[t * TILE : (t + 1) * TILE, cols])
    own_terms = [[key_terms(t, p) for p in range(pairs)] for t in range(tiles)]
    dq_t = jnp.concatenate(
        [mm(kt[h * HD : (h + 1) * HD, :], sb[:, h * rows : (h + 1) * rows]) for h in range(heads)], axis=0
    )
    dq_ref[...] = (jnp.transpose(dq_t) * scale).astype(BF16)


    for side in range(2):
        @pl.when(has[side])
        def _():
            grad_wait(side).wait_recv()
    for t in range(tiles):
        lines = slice(t * TILE, (t + 1) * TILE)
        gates = [jnp.where(chosen[side] == t, 1.0, 0.0).astype(F32) for side in range(2)]
        for p in range(pairs):
            cols = slice(p * LANES, (p + 1) * LANES)
            for which, out in ((0, dk_ref), (1, dv_ref)):
                value = own_terms[t][p][which]
                for side in range(2):
                    value = value + grecv[side, which, :, cols].astype(F32) * gates[side]
                out[lines, cols] = value.astype(BF16)

    for i in range(nx):
        along_z(functools.partial(forward_part, i), owners, near)
    for i in range(nx):
        cols = pl.ds(pl.multiple_of(on_x(i) * feats, feats), feats)
        for j in range(owners):
            start = j * piece
            wg_ref[pl.ds(pl.multiple_of(c * half + start, piece), piece), cols] = ag[i, c, j]
    for d in range(1, ns):
        other = on_sub(d)
        for i in range(nx):
            cols = pl.ds(pl.multiple_of(on_x(i) * feats, feats), feats)
            for j in range(owners):
                remote(
                    ag.at[i, c, j], ag.at[i, other, j], f_send.at[i, d - 1, j], f_recv.at[i, other, j], {"sub": other}
                ).wait_recv()
                start = j * piece
                wg_ref[pl.ds(pl.multiple_of(other * half + start, piece), piece), cols] = ag[i, other, j]
    for side in range(2):
        @pl.when(has[side])
        def _():
            for which in range(2):
                halo_copy(side, which).wait_send()
            grad_copy(side).wait_send()
    for copy in x_copies:
        copy.wait_send()
    for i in range(nx):
        for d in range(1, ns):
            pair_copy(d, i).wait_send()
        along_z(lambda j: piece_out(i, j).wait_send(), owners, far)

    def owner_sent():
        for i in range(nx):
            along_z(lambda j: to_owner_peer(i, j).wait_send(), nz, far)

    if owners == nz:
        owner_sent()
    else:
        pl.when(z < owners)(owner_sent)
    for i in range(nx):
        for d in range(1, ns):
            for j in range(owners):
                to_core(i, j, d).wait_send()


def deliver(dq_ref, dk_ref, dv_ref, wg_ref, dq_out, dk_out, dv_out, wg_out, wide, sem):
    copies = [
        pltpu.make_async_copy(dq_ref, dq_out, sem.at[0]),
        pltpu.make_async_copy(dk_ref, dk_out, sem.at[1]),
        pltpu.make_async_copy(dv_ref, dv_out, sem.at[2]),
        pltpu.make_async_copy(wide, wg_out, sem.at[3]),
    ]
    for copy in copies[:3]:
        copy.start()
    wide[...] = wg_ref[...].astype(F32)
    copies[3].start()
    for copy in copies:
        copy.wait()


def solution(mesh):
    nz, nx, ns = mesh.shape["nodes"], mesh.shape["heads"], mesh.shape["sub"]

    def on_device(
        queries, key_vectors, value_vectors, cotangent, out_weight, neighbours, entry_mask, live_counts, tile_slot
    ):
        rows, feats = queries.shape
        width = out_weight.shape[1]
        tiles, heads = rows // TILE, feats // HD
        keys = (tiles + 2) * TILE
        half = feats // ns
        owners = min(nz, half // 16)
        piece = half // owners
        vmem, hbm = pl.BlockSpec(memory_space=pltpu.VMEM), pl.BlockSpec(memory_space=pltpu.HBM)
        dma = pltpu.SemaphoreType.DMA
        partial = pl.pallas_call(
            functools.partial(kernel, (nz, nx, ns, owners)),
            out_shape=(
                jax.ShapeDtypeStruct((rows, feats), BF16),
                jax.ShapeDtypeStruct((rows, feats), BF16),
                jax.ShapeDtypeStruct((rows, feats), BF16),
                jax.ShapeDtypeStruct((feats, width), BF16),
            ),
            in_specs=[hbm] * 9,
            out_specs=(vmem,) * 4,
            scratch_shapes=[
                pltpu.SMEM(neighbours.shape, jnp.int32),
                pltpu.SMEM(entry_mask.shape, jnp.int32),
                pltpu.SMEM(live_counts.shape, jnp.int32),
                pltpu.SMEM(tile_slot.shape, jnp.int32),
                pltpu.VMEM((rows, feats), BF16),
                pltpu.VMEM((rows, feats), BF16),
                pltpu.VMEM((rows, feats), BF16),
                pltpu.VMEM((feats, width), BF16),
                dma((9,)),
                pltpu.VMEM((nx, rows, feats), BF16),
                pltpu.VMEM((2, 2, TILE, feats), BF16),
                pltpu.VMEM((2, 2, TILE, feats), BF16),
                pltpu.VMEM((2, 2, TILE, feats), BF16),
                pltpu.VMEM((2, 2, TILE, feats), BF16),
                pltpu.VMEM((heads, LANES, rows), BF16),
                pltpu.VMEM((heads, rows, LANES), BF16),
                pltpu.VMEM((heads, LANES, rows), BF16),
                pltpu.VMEM((heads, rows, LANES), BF16),
                pltpu.VMEM((feats, keys), BF16),
                pltpu.VMEM((feats, keys), BF16),
                pltpu.VMEM((feats, rows), BF16),
                pltpu.VMEM((heads, keys, rows), F32),
                pltpu.VMEM((keys, heads * rows), BF16),
                pltpu.VMEM((keys, heads * rows), BF16),
                pltpu.VMEM((ns - 1, nx, half, feats), BF16),
                pltpu.VMEM((ns - 1, nx, half, feats), BF16),
                pltpu.VMEM((nx, owners, piece, feats), BF16),
                pltpu.VMEM((nx, nz, piece, feats), BF16),
                pltpu.VMEM((nx, ns, owners, piece, feats), BF16),
                pltpu.VMEM((2, heads, 1, rows), F32),
                dma((nx,)), dma((nx,)),
                dma((2, 2)), dma((2, 2)),
                dma((2,)), dma((2,)),
                dma((ns - 1, nx)), dma((ns - 1, nx)),
                dma((nx, owners)), dma((nx, nz)),
                dma((nx, nz)), dma((nx, owners)),
                dma((nx, ns - 1, owners)), dma((nx, ns, owners)),
            ],
            compiler_params=pltpu.CompilerParams(
                collective_id=0, has_side_effects=True, vmem_limit_bytes=48 * 1024 * 1024
            ),
        )(
            *(
                pltpu.with_memory_space_constraint(array, pltpu.HBM)
                for array in (
                    neighbours, entry_mask, live_counts, tile_slot,
                    queries, key_vectors, value_vectors, cotangent, out_weight,
                )
            )
        )
        return pl.pallas_call(
            deliver,
            out_shape=(
                jax.ShapeDtypeStruct((rows, feats), BF16),
                jax.ShapeDtypeStruct((rows, feats), BF16),
                jax.ShapeDtypeStruct((rows, feats), BF16),
                jax.ShapeDtypeStruct((feats, width), F32),
            ),
            in_specs=[vmem] * 4,
            out_specs=(hbm,) * 4,
            scratch_shapes=[pltpu.VMEM((feats, width), F32), dma((4,))],
            compiler_params=pltpu.CompilerParams(vmem_limit_bytes=4 * 1024 * 1024),
        )(*partial)

    part = P(("groups", "nodes", "sub"), "heads")
    return jax.shard_map(
        on_device,
        mesh=mesh,
        in_specs=(
            part, part, part, part, P("heads", None), P("groups", None), P("groups", None), P("groups"), P("groups"),
        ),
        out_specs=(part, part, part, P(("groups", "heads"), None)),
        check_vma=False,
    )
```
